256 devices in a mesh: seq: 128 (over x_lo, z, y, core), tp: 2 (over x_hi).
Axes of the slice: x: 4 (x_hi: 2, x_lo: 2; x = x_hi * 2 + x_lo), y: 4, z: 8, core: 2. Of those that a mesh axis runs over, the one named last changes fastest.
Arguments:
- tokens: bfloat16 [32768, 1024], P('seq', 'tp')
- w_query: bfloat16 [1024, 1024], P(None, 'tp'), may hold values from -0.1875 to 0.1875
- w_key: bfloat16 [1024, 1024], P(None, 'tp'), may hold values from -0.1875 to 0.1875
- w_value: bfloat16 [1024, 1024], P(None, 'tp'), may hold values from -0.1875 to 0.1875
- w_out: bfloat16 [1024, 1024], P('tp'), may hold values from -0.1875 to 0.1875
- grad_out: bfloat16 [32768, 1024], P('seq', 'tp'), may hold values from -6 to 6
- block_sky: int32 [128], replicated, may hold values from 0 to 127, as said below
- neighbours: int32 [128, 3], replicated, may hold values from 0 to 127, as said below
- valid_count: int32 [128], replicated, may hold values from 32 to 256
Outputs:
- outputs: bfloat16 [32768, 1024], P('seq', 'tp')
- input_grads: bfloat16 [32768, 1024], P('seq', 'tp')
The draws below stay inside these ranges and needn't reach their ends.
Inputs may be any that keep to these rules, and one draw needn't show every extreme that they name: `block_sky`: a permutation; slot s lies on the seq index s. Three different sky blocks other than the block itself; for the block in slot s the slots of its neighbours lie on three different seq indices at distance 1 or 2 from that of slot s, counted modulo the size of seq.
All inputs are finite; a program needn't handle non-finite values.
Results may differ from the reference program's by a relative error of at most 0.018.
The reference program's roundings to bfloat16 on the way (of `weights`, `attended`, `grad_rows`, `score_grads` and `query_grads`) count: a program that leaves them out, or rounds other values in their place, can miss the bound.
Values may be sent and summed in bfloat16 or wider, within the bound.
A program may use at most 128 MiB of HBM per device.

```python
import jax
import jax.numpy as jnp
import numpy as np
from jax import lax

D = 1024
H = 16
HD = 64
BLK = 256
BLK_DEV = 1
NB = 128
TOKENS = 32768


def draw_tokens(key, part):
    base = jax.random.normal(key, (TOKENS, D), jnp.float32)
    values = jnp.clip(base, -6.0, 6.0)
    return values.astype(jnp.bfloat16)


def sky_layout(key):
    seeded = jax.random.fold_in(key, 17)
    placement = jax.random.permutation(jax.random.fold_in(seeded, 1), NB).astype(jnp.int32)
    dropped = jax.random.randint(jax.random.fold_in(seeded, 2), (NB,), 0, 4)
    table = jnp.array(np.array([[-1, 1, 2], [-2, 1, 2], [-2, -1, 2], [-2, -1, 1]], np.int32))
    offsets = table[dropped]
    inner = jax.random.randint(jax.random.fold_in(seeded, 3), (NB, 3), 0, BLK_DEV)
    slot_ids = jnp.arange(NB, dtype=jnp.int32)
    device_count = NB // BLK_DEV
    near = (slot_ids[:, None] // BLK_DEV + offsets) % device_count * BLK_DEV + inner
    neighbour_sky = jnp.zeros((NB, 3), jnp.int32).at[placement].set(placement[near])
    return (placement, neighbour_sky)


def draw_block_sky(key, part):
    return sky_layout(key)[0]


def draw_neighbours(key, part):
    return sky_layout(key)[1]


def draw_valid_count(key, part):
    counts = jax.random.randint(jax.random.fold_in(key, 5), (NB,), BLK // 8, BLK + 1)
    full = jnp.arange(NB, dtype=jnp.int32) % 4 == 0
    return jnp.where(full, BLK, counts).astype(jnp.int32)


def block_levels(key, extent, pieces, least, high):
    loudness = 1.0
    for dim, shards_of in pieces:
        steps = jax.random.uniform(jax.random.fold_in(jax.random.fold_in(key, 6), dim), (shards_of,), jnp.float32, least / len(pieces), high / len(pieces))
        loudness = loudness * jnp.repeat(jnp.exp(steps), extent[dim] // shards_of).reshape((-1,) + (1,) * (len(extent) - 1 - dim))
    return loudness


def gaussian(rng, extent, deviation, bound, cuts=(), held_as=jnp.bfloat16):
    factor_of = block_levels(rng, extent, cuts, -0.22, 0.18) if cuts else 1.0
    values = jax.random.normal(rng, extent, jnp.float32) * deviation * factor_of
    return jnp.minimum(jnp.maximum(values, -bound), bound).astype(held_as)


def setup_inputs(seed: int = 0) -> dict:
    splits = jax.random.split(jax.random.key(seed), 10)
    tokens = draw_tokens(jax.random.fold_in(splits[9], 71), 0)
    w_query = gaussian(splits[1], (D, D), D ** -0.5, 0.1875, ((1, 2),))
    w_key = gaussian(splits[2], (D, D), D ** -0.5, 0.1875, ((1, 2),))
    w_value = gaussian(splits[3], (D, D), D ** -0.5, 0.1875, ((1, 2),))
    w_out = gaussian(splits[4], (D, D), D ** -0.5, 0.1875, ((0, 2),))
    grad_out = gaussian(splits[5], (TOKENS, D), 1.0, 6.0, ((0, 128), (1, 2)))
    block_sky = draw_block_sky(jax.random.fold_in(splits[9], 71), 0)
    neighbours = draw_neighbours(jax.random.fold_in(splits[9], 71), 0)
    valid_count = draw_valid_count(jax.random.fold_in(splits[9], 71), 0)
    return {"tokens": tokens, "w_query": w_query, "w_key": w_key, "w_value": w_value, "w_out": w_out, "grad_out": grad_out, "block_sky": block_sky, "neighbours": neighbours, "valid_count": valid_count}


def reference(tokens, w_query, w_key, w_value, w_out, grad_out, block_sky, neighbours, valid_count):
    blocks = block_sky.shape[0]
    rows_all = tokens.shape[0]
    scale = HD ** -0.5

    def project(weight):
        return jnp.dot(tokens, weight, preferred_element_type=jnp.float32).astype(jnp.bfloat16)

    queries = project(w_query)
    key_rows = project(w_key)
    value_rows = project(w_value)
    numbers = jnp.arange(blocks, dtype=jnp.int32)
    slot_of = jnp.zeros((blocks,), jnp.int32).at[block_sky].set(numbers)
    near_slots = slot_of[neighbours[block_sky]]
    key_slots = jnp.concatenate([numbers[:, None], near_slots], axis=1).astype(jnp.int32)
    key_counts = valid_count[block_sky[key_slots]]
    positions = jnp.arange(BLK, dtype=jnp.int32)
    key_mask = (positions[None, None, :] < key_counts[:, :, None]).reshape(blocks, 4 * BLK)
    q_blocks = queries.reshape(blocks, BLK, H, HD)
    k_blocks = key_rows.reshape(blocks, BLK, H, HD)
    v_blocks = value_rows.reshape(blocks, BLK, H, HD)

    def scores_for(slot):
        keys_here = k_blocks[key_slots[slot]].reshape(4 * BLK, H, HD).astype(jnp.float32)
        values_here = v_blocks[key_slots[slot]].reshape(4 * BLK, H, HD).astype(jnp.float32)
        rows_here = q_blocks[slot].astype(jnp.float32)
        scores = jnp.einsum("qhd,khd->hqk", rows_here, keys_here) * scale
        scores = jnp.where(key_mask[slot][None, None, :], scores, -jnp.inf)
        return scores, rows_here, keys_here, values_here

    def forward(slot):
        scores, rows_here, keys_here, values_here = scores_for(slot)
        row_max = jnp.max(scores, axis=-1, keepdims=True)
        log_total = row_max + jnp.log(jnp.sum(jnp.exp(scores - row_max), axis=-1, keepdims=True))
        weights = jnp.exp(scores - log_total).astype(jnp.bfloat16)
        attended = jnp.einsum("hqk,khd->qhd", weights.astype(jnp.float32), values_here).astype(jnp.bfloat16)
        return attended, log_total[:, :, 0]

    attended, log_totals = lax.map(forward, numbers)
    attended = attended.reshape(rows_all, D)
    outputs = jnp.dot(attended, w_out, preferred_element_type=jnp.float32).astype(jnp.bfloat16)
    grad_rows = jnp.dot(grad_out, w_out.T, preferred_element_type=jnp.float32).astype(jnp.bfloat16)
    g_blocks = grad_rows.reshape(blocks, BLK, H, HD)

    def backward(carry, slot):
        key_acc, value_acc = carry
        scores, rows_here, keys_here, values_here = scores_for(slot)
        probabilities = jnp.exp(scores - log_totals[slot][:, :, None])
        weights = probabilities.astype(jnp.bfloat16)
        grads_here = g_blocks[slot].astype(jnp.float32)
        prob_grads = jnp.einsum("qhd,khd->hqk", grads_here, values_here)
        row_delta = jnp.sum(probabilities * prob_grads, axis=-1)
        score_grads = (probabilities * (prob_grads - row_delta[:, :, None]) * scale).astype(jnp.bfloat16)
        row_grads = jnp.einsum("hqk,khd->qhd", score_grads.astype(jnp.float32), keys_here).astype(jnp.bfloat16)
        key_part = jnp.einsum("hqk,qhd->khd", score_grads.astype(jnp.float32), rows_here).reshape(4, BLK, H, HD)
        value_part = jnp.einsum("hqk,qhd->khd", weights.astype(jnp.float32), grads_here).reshape(4, BLK, H, HD)
        key_acc = key_acc.at[key_slots[slot]].add(key_part)
        value_acc = value_acc.at[key_slots[slot]].add(value_part)
        return (key_acc, value_acc), row_grads

    start = (jnp.zeros((blocks, BLK, H, HD), jnp.float32), jnp.zeros((blocks, BLK, H, HD), jnp.float32))
    (key_acc, value_acc), query_grads = lax.scan(backward, start, numbers)
    query_grads = query_grads.reshape(rows_all, D)
    key_grads = key_acc.reshape(rows_all, D).astype(jnp.bfloat16)
    value_grads = value_acc.reshape(rows_all, D).astype(jnp.bfloat16)
    summed = jnp.dot(query_grads, w_query.T, preferred_element_type=jnp.float32)
    summed = summed + jnp.dot(key_grads, w_key.T, preferred_element_type=jnp.float32)
    summed = summed + jnp.dot(value_grads, w_value.T, preferred_element_type=jnp.float32)
    return outputs, summed.astype(jnp.bfloat16)
```

```python
import functools

import jax
import jax.numpy as jnp
from jax import lax
from jax.experimental import pallas as pl
from jax.experimental.pallas import tpu as pltpu
from jax.sharding import PartitionSpec as P

MESH = pl.DeviceIdType.MESH
BLK = 256
PAIR = 128
NP = 4
HALF = 512
F32 = jnp.float32
BF16 = jnp.bfloat16

SIB, NEAR, FAR, CROSS = 0, 1, 2, 3


def dot(a, b):
    return jnp.dot(a, b, preferred_element_type=F32)


def dot_nt(a, b):
    return lax.dot_general(a, b, (((1,), (1,)), ((), ())), preferred_element_type=F32)


def dot_tn(a, b):
    return lax.dot_general(a, b, (((0,), (0,)), ((), ())), preferred_element_type=F32)


def pick(cond, a, b):
    return lax.select_n(cond, b, a)


def kernel(
    n,
    tok_hbm, wq_hbm, wk_hbm, wv_hbm, wo_hbm, go_hbm, sky_ref, nb_ref, vc_ref,
    out_ref, ig_ref,
    tok, tokp, go, gop, wq, wk, wv, wo, acc,
    kv_own, win, q2, g2, bias, kc, vc, s_ref, d_ref, p_ref, ds_ref,
    att, dq, own_g, near_g, gsib, gfar, gnear, rsib, rnear, rfar, dk, dv,
    osend, orecv, isend, irecv,
    lsem, tp_ssem, tp_rsem, kv_ssem, kv_rsem, g_ssem, g_rsem,
):
    s = lax.axis_index("seq")
    t = lax.axis_index("tp")
    sgn = 1 - 2 * (s % 2)

    def dev(offset):
        return ((s + sgn * offset + n) % n, t)

    sib, near, far, peer = dev(1), dev(2), dev(-2), (s, 1 - t)

    def remote(src, dst, ssem, rsem, to):
        return pltpu.make_async_remote_copy(
            src_ref=src, dst_ref=dst, send_sem=ssem, recv_sem=rsem, device_id=to, device_id_type=MESH
        )

    def local(i, src, dst):
        return pltpu.make_async_copy(src, dst, lsem.at[i])

    loads = [
        local(0, tok_hbm, tok),
        local(1, wk_hbm, wk),
        local(2, wv_hbm, wv),
        local(3, wq_hbm, wq),
        local(4, go_hbm, go),
        local(5, wo_hbm, wo),
    ]
    for copy in loads:
        copy.start()

    barrier = pltpu.get_barrier_semaphore()
    for to in (peer, sib, near, far):
        pl.semaphore_signal(barrier, inc=1, device_id=to, device_id_type=MESH)
    pl.semaphore_wait(barrier, 4)

    def tp_copy(i, src, dst):
        return remote(src, dst, tp_ssem.at[i], tp_rsem.at[i], peer)

    tok_copy = tp_copy(0, tok_hbm, tokp)
    go_copy = tp_copy(1, go_hbm, gop)
    out_copy = tp_copy(2, osend, orecv)
    in_copy = tp_copy(3, isend, irecv)
    tok_copy.start()
    go_copy.start()

    def kv_copy(o, p):
        src = win.at[NEAR, p] if o == CROSS else kv_own.at[p]
        to = {SIB: sib, NEAR: far, FAR: near, CROSS: sib}[o]
        return remote(src, win.at[o, p], kv_ssem.at[o, p], kv_rsem.at[o, p], to)

    def sib_copy(p):
        return remote(gsib.at[p], rsib.at[p], g_ssem.at[0, p], g_rsem.at[0, p], sib)

    def far_copy(p):
        return remote(gfar.at[p], rnear.at[p], g_ssem.at[1, p], g_rsem.at[1, p], far)

    def near_copy(p):
        return remote(gnear.at[p], rfar.at[p], g_ssem.at[2, p], g_rsem.at[2, p], near)

    own_sky = sky_ref[s]
    near_sky = [nb_ref[own_sky, j] for j in range(3)]

    def around(offset):
        sky = sky_ref[(s + sgn * offset + n) % n]
        here = (sky == near_sky[0]) | (sky == near_sky[1]) | (sky == near_sky[2])
        return here, vc_ref[sky]

    own_count = vc_ref[own_sky]
    has_far, far_count = around(-2)
    has_cross, cross_count = around(-1)
    _, sib_count = around(1)
    has_near, near_count = around(2)
    c0 = has_far
    c1 = has_far & has_cross
    c2 = jnp.logical_not(has_near)
    counts = (
        own_count,
        jnp.where(c0, far_count, cross_count),
        jnp.where(c1, cross_count, sib_count),
        jnp.where(c2, sib_count, near_count),
    )
    rows = lax.broadcasted_iota(jnp.int32, (BLK, PAIR), 0)
    for j in range(4):
        bias[j * BLK : (j + 1) * BLK, :] = jnp.where(rows < counts[j], 0.0, -jnp.inf).astype(F32)

    own_rows = pl.ds(pl.multiple_of(t * HALF, HALF), HALF)
    peer_rows = pl.ds(pl.multiple_of((1 - t) * HALF, HALF), HALF)

    loads[0].wait()
    loads[1].wait()
    acc[0] = dot(tok[...], wk[own_rows, :])
    loads[2].wait()
    acc[1] = dot(tok[...], wv[own_rows, :])
    loads[3].wait()
    acc[2] = dot(tok[...], wq[own_rows, :])
    tok_copy.wait_recv()
    for half in range(2):
        cols = slice(half * 256, half * 256 + 256)
        for j, w in ((0, wk), (1, wv)):
            value = (acc[j, :, cols] + dot(tokp[...], w[peer_rows, cols])).astype(BF16)
            kv_own[2 * half, j] = value[:, :PAIR]
            kv_own[2 * half + 1, j] = value[:, PAIR:]
        for p in (2 * half, 2 * half + 1):
            for o in (NEAR, FAR, SIB):
                kv_copy(o, p).start()

    first = lax.broadcasted_iota(jnp.int32, (BLK, PAIR), 1) < 64

    def split(ref, value):
        for p in range(NP):
            part = value[:, p * PAIR : (p + 1) * PAIR]
            ref[p, :BLK, :] = jnp.where(first, part, 0.0).astype(BF16)
            ref[p, BLK:, :] = jnp.where(first, 0.0, part).astype(BF16)

    split(q2, (acc[2] + dot(tokp[...], wq[peer_rows, :])) * 0.125)
    loads[4].wait()
    loads[5].wait()
    acc[0] = dot_nt(go[...], wo[:, own_rows])
    go_copy.wait_recv()
    split(g2, acc[0] + dot_nt(gop[...], wo[:, peer_rows]))

    def forward_near(p):
        kv_copy(NEAR, p).wait_recv()
        kv_copy(CROSS, p).start()

    def combine_near(p):
        sib_copy(p).wait_recv()
        for j in range(2):
            gnear[p, j] = (near_g[p, j] + rsib[p, 1, j].astype(F32)).astype(BF16)
        near_copy(p).start()

    def pair_step(p):
        kv_copy(SIB, p).wait_recv()
        kv_copy(FAR, p).wait_recv()
        kv_copy(CROSS, p).wait_recv()
        for j, ref in ((0, kc), (1, vc)):
            ref[0:256, :] = kv_own[p, j]
            ref[256:512, :] = pick(c0, win[FAR, p, j], win[CROSS, p, j])
            ref[512:768, :] = pick(c1, win[CROSS, p, j], win[SIB, p, j])
            ref[768:1024, :] = pick(c2, win[SIB, p, j], win[NEAR, p, j])
        q = q2[p]
        g = g2[p]
        for k in range(4):
            ks = slice(k * BLK, (k + 1) * BLK)
            b = bias[ks, :]
            s_ref[ks, :] = dot_nt(kc[ks, :], q) + jnp.concatenate([b, b, b, b], axis=1)
            d_ref[ks, :] = dot_nt(vc[ks, :], g)
        for c in range(4):
            cols = slice(c * 128, (c + 1) * 128)
            top = jnp.max(s_ref[:, cols], axis=0, keepdims=True)
            total = jnp.zeros((8, 128), F32)
            mixed = jnp.zeros((8, 128), F32)
            for k in range(8):
                ks = slice(k * 128, (k + 1) * 128)
                e = jnp.exp(s_ref[ks, cols] - top)
                s_ref[ks, cols] = e
                total = total + jnp.sum(e.reshape(16, 8, 128), axis=0)
                mixed = mixed + jnp.sum((e * d_ref[ks, cols]).reshape(16, 8, 128), axis=0)
            inverse = 1.0 / jnp.sum(total, axis=0, keepdims=True)
            delta = jnp.sum(mixed, axis=0, keepdims=True) * inverse
            for k in range(8):
                ks = slice(k * 128, (k + 1) * 128)
                prob = s_ref[ks, cols] * inverse
                p_ref[ks, cols] = prob.astype(BF16)
                ds_ref[ks, cols] = (prob * (d_ref[ks, cols] - delta)).astype(BF16)

        def parts(j, left, right):
            def block(b):
                return dot(left[b * BLK : (b + 1) * BLK, :], right)

            own_g[p, j] = block(0)
            a, b, c = block(1), block(2), block(3)
            zero = jnp.zeros_like(a)
            gfar[p, j] = pick(c0, a, zero).astype(BF16)
            gsib[p, 1, j] = pick(c0, pick(c1, b, zero), a).astype(BF16)
            gsib[p, 0, j] = pick(c1, pick(c2, c, zero), b).astype(BF16)
            near_g[p, j] = pick(c2, zero, c)

        parts(0, ds_ref, q)
        parts(1, p_ref, g)
        sib_copy(p).start()
        far_copy(p).start()
        lanes = pl.ds(pl.multiple_of(p * PAIR, PAIR), PAIR)
        for source, left, ref, scale in ((p_ref, vc, att, 1.0), (ds_ref, kc, dq, 0.125)):
            both = dot_tn(left[...], source[...])
            joined = jnp.concatenate([both[:64, :BLK], both[64:, BLK:]], axis=0) * scale
            ref[:, lanes] = joined.T.astype(BF16)

    forward_near(0)

    @pl.loop(0, NP)
    def _(p):
        @pl.when(p + 1 < NP)
        def _():
            forward_near(p + 1)

        pair_step(p)
        combine_near(p)

    osend[...] = dot(att[...], wo[:, peer_rows]).astype(BF16)
    out_copy.start()
    acc[0] = dot(att[...], wo[:, own_rows])
    acc[1] = dot_nt(dq[...], wq[peer_rows, :])
    acc[2] = dot_nt(dq[...], wq[own_rows, :])

    for p in range(NP):
        far_copy(p).wait_recv()
        near_copy(p).wait_recv()
        lanes = slice(p * PAIR, (p + 1) * PAIR)
        for j, ref in ((0, dk), (1, dv)):
            summed = own_g[p, j] + rsib[p, 0, j].astype(F32)
            summed = summed + rnear[p, j].astype(F32) + rfar[p, j].astype(F32)
            ref[:, lanes] = summed.astype(BF16)
    isend[...] = (
        acc[1] + dot_nt(dk[...], wk[peer_rows, :]) + dot_nt(dv[...], wv[peer_rows, :])
    ).astype(BF16)
    in_copy.start()
    out_copy.wait_recv()
    out_ref[...] = (acc[0] + orecv[...].astype(F32)).astype(BF16)
    acc[1] = acc[2] + dot_nt(dk[...], wk[own_rows, :]) + dot_nt(dv[...], wv[own_rows, :])
    in_copy.wait_recv()
    ig_ref[...] = (acc[1] + irecv[...].astype(F32)).astype(BF16)

    for copy in (tok_copy, go_copy, out_copy, in_copy):
        copy.wait_send()
    for p in range(NP):
        for o in range(4):
            kv_copy(o, p).wait_send()
        for copy in (sib_copy(p), far_copy(p), near_copy(p)):
            copy.wait_send()


def body(n, *args):
    wide = (BLK, HALF)
    half = pltpu.VMEM(wide, BF16)
    weight = pltpu.VMEM((2 * HALF, HALF), BF16)
    pair_kv = pltpu.VMEM((NP, 2, BLK, PAIR), BF16)
    pair_f32 = pltpu.VMEM((NP, 2, BLK, PAIR), F32)
    sib_kv = pltpu.VMEM((NP, 2, 2, BLK, PAIR), BF16)
    scratch = [
        half, half, half, half, weight, weight, weight, pltpu.VMEM((HALF, 2 * HALF), BF16),
        pltpu.VMEM((3,) + wide, F32),
        pair_kv, pltpu.VMEM((4, NP, 2, BLK, PAIR), BF16),
        pltpu.VMEM((NP, 2 * BLK, PAIR), BF16), pltpu.VMEM((NP, 2 * BLK, PAIR), BF16),
        pltpu.VMEM((4 * BLK, PAIR), F32),
        pltpu.VMEM((4 * BLK, PAIR), BF16), pltpu.VMEM((4 * BLK, PAIR), BF16),
        pltpu.VMEM((4 * BLK, 2 * BLK), F32), pltpu.VMEM((4 * BLK, 2 * BLK), F32),
        pltpu.VMEM((4 * BLK, 2 * BLK), BF16), pltpu.VMEM((4 * BLK, 2 * BLK), BF16),
        half, half, pair_f32, pair_f32, sib_kv, pair_kv, pair_kv, sib_kv, pair_kv, pair_kv, half, half,
        half, half, half, half,
        pltpu.SemaphoreType.DMA((6,)),
        pltpu.SemaphoreType.DMA((4,)), pltpu.SemaphoreType.DMA((4,)),
        pltpu.SemaphoreType.DMA((4, NP)), pltpu.SemaphoreType.DMA((4, NP)),
        pltpu.SemaphoreType.DMA((3, NP)), pltpu.SemaphoreType.DMA((3, NP)),
    ]
    shape = jax.ShapeDtypeStruct(wide, BF16)
    return pl.pallas_call(
        functools.partial(kernel, n),
        name="sky_attention",
        out_shape=(shape, shape),
        in_specs=[pl.BlockSpec(memory_space=pl.ANY)] * 6 + [pl.BlockSpec(memory_space=pltpu.SMEM)] * 3,
        out_specs=[pl.BlockSpec(memory_space=pltpu.VMEM)] * 2,
        scratch_shapes=scratch,
        compiler_params=pltpu.CompilerParams(
            collective_id=0, has_side_effects=True, vmem_limit_bytes=48 << 20
        ),
    )(*args)


def solution(mesh):
    placed = (
        P("seq", "tp"),
        P(None, "tp"),
        P(None, "tp"),
        P(None, "tp"),
        P("tp", None),
        P("seq", "tp"),
        P(),
        P(),
        P(),
    )
    return jax.shard_map(
        functools.partial(body, mesh.shape["seq"]),
        mesh=mesh,
        in_specs=placed,
        out_specs=(P("seq", "tp"), P("seq", "tp")),
        check_vma=False,
    )
```

```python
import functools

import jax
import jax.numpy as jnp
from jax import lax
from jax.experimental import pallas as pl
from jax.experimental.pallas import tpu as pltpu
from jax.sharding import PartitionSpec as P

MESH = pl.DeviceIdType.MESH
BLK = 256
PAIR = 128
NP = 4
HALF = 512
F32 = jnp.float32
BF16 = jnp.bfloat16

SIB, NEAR, FAR, CROSS = 0, 1, 2, 3
KV_RELAYED = (1, 3)
G_RELAYED = (0, 2)


def dot(a, b):
    return jnp.dot(a, b, preferred_element_type=F32)


def dot_nt(a, b):
    return lax.dot_general(a, b, (((1,), (1,)), ((), ())), preferred_element_type=F32)


def dot_tn(a, b):
    return lax.dot_general(a, b, (((0,), (0,)), ((), ())), preferred_element_type=F32)


def pick(cond, a, b):
    return lax.select_n(cond, b, a)


def kernel(
    n,
    tok_hbm, wq_hbm, wk_hbm, wv_hbm, wo_hbm, go_hbm, sky_ref, nb_ref, vc_ref,
    out_ref, ig_ref,
    tok, tokp, go, gop, wq, wk, wv, wo, acc,
    kv_own, win, q2, g2, bias, kc, vc, s_ref, d_ref, p_ref, ds_ref,
    att, dq, own_g, near_g, gsib, gfar, gnear, rsib, rnear, rfar, dk, dv,
    osend, orecv, isend, irecv, kv_relay, g_relay,
    relay_ssem, relay_rsem, lsem, tp_ssem, tp_rsem, kv_ssem, kv_rsem, g_ssem, g_rsem,
):
    s = lax.axis_index("seq")
    t = lax.axis_index("tp")
    sgn = 1 - 2 * (s % 2)

    def dev(offset):
        return ((s + sgn * offset + n) % n, t)

    sib, near, far, peer = dev(1), dev(2), dev(-2), (s, 1 - t)

    half_n = n // 2
    right_end = s % half_n >= half_n - 2
    left_end = s % half_n < 2
    even = s % 2 == 0
    near_crosses = (even & right_end) | (jnp.logical_not(even) & left_end)
    far_crosses = (even & left_end) | (jnp.logical_not(even) & right_end)
    at_end = right_end | left_end
    step = jnp.where(right_end, 2, -2)
    partner = ((s + half_n) % n, t)
    partners_end = ((s + half_n + step + n) % n, t)

    def remote(src, dst, ssem, rsem, to):
        return pltpu.make_async_remote_copy(
            src_ref=src, dst_ref=dst, send_sem=ssem, recv_sem=rsem, device_id=to, device_id_type=MESH
        )

    def local(i, src, dst):
        return pltpu.make_async_copy(src, dst, lsem.at[i])

    loads = [
        local(0, tok_hbm, tok),
        local(1, wk_hbm, wk),
        local(2, wv_hbm, wv),
        local(3, wq_hbm, wq),
        local(4, go_hbm, go),
        local(5, wo_hbm, wo),
    ]
    for copy in loads:
        copy.start()

    barrier = pltpu.get_barrier_semaphore()
    for to in (peer, sib, near, far):
        pl.semaphore_signal(barrier, inc=1, device_id=to, device_id_type=MESH)

    @pl.when(at_end)
    def _():
        for to in (partner, partners_end):
            pl.semaphore_signal(barrier, inc=1, device_id=to, device_id_type=MESH)
        pl.semaphore_wait(barrier, 6)

    @pl.when(jnp.logical_not(at_end))
    def _():
        pl.semaphore_wait(barrier, 4)


    def tp_copy(i, src, dst):
        return remote(src, dst, tp_ssem.at[i], tp_rsem.at[i], peer)

    tok_copy = tp_copy(0, tok_hbm, tokp)
    go_copy = tp_copy(1, go_hbm, gop)
    out_copy = tp_copy(2, osend, orecv)
    in_copy = tp_copy(3, isend, irecv)
    tok_copy.start()
    go_copy.start()

    def kv_copy(o, p):
        src = win.at[NEAR, p] if o == CROSS else kv_own.at[p]
        to = {SIB: sib, NEAR: far, FAR: near, CROSS: sib}[o]
        return remote(src, win.at[o, p], kv_ssem.at[o, p], kv_rsem.at[o, p], to)

    def sib_copy(p):
        return remote(gsib.at[p], rsib.at[p], g_ssem.at[0, p], g_rsem.at[0, p], sib)

    def far_copy(p):
        return remote(gfar.at[p], rnear.at[p], g_ssem.at[1, p], g_rsem.at[1, p], far)

    def near_copy(p):
        return remote(gnear.at[p], rfar.at[p], g_ssem.at[2, p], g_rsem.at[2, p], near)

    class Crossing:
        def __init__(self, crosses, direct, first, second):
            self.crosses, self.direct, self.first, self.second = crosses, direct, first, second

        def start(self):
            pl.when(self.crosses)(lambda: self.first().start())
            pl.when(jnp.logical_not(self.crosses))(lambda: self.direct().start())

        def pass_on(self):
            @pl.when(self.crosses)
            def _():
                self.first().wait_recv()
                self.second().start()

        def wait_send(self):
            @pl.when(self.crosses)
            def _():
                self.first().wait_send()
                self.second().wait_send()

            pl.when(jnp.logical_not(self.crosses))(lambda: self.direct().wait_send())

    def crossing(crosses, i, direct, src, buffer, dst, sem):
        return Crossing(
            crosses,
            direct,
            lambda: remote(src, buffer, relay_ssem.at[i], relay_rsem.at[i], partner),
            lambda: remote(buffer, dst, relay_ssem.at[i + 4], sem, partners_end),
        )

    def kv_crossing(o, i):
        p = KV_RELAYED[i]
        return crossing(
            near_crosses if o == FAR else far_crosses, i, lambda: kv_copy(o, p),
            kv_own.at[p], kv_relay.at[i], win.at[o, p], kv_rsem.at[o, p],
        )

    def g_crossing(is_near, i):
        p = G_RELAYED[i]
        if is_near:
            return crossing(
                near_crosses, i + 2, lambda: near_copy(p),
                gnear.at[p], g_relay.at[i], rfar.at[p], g_rsem.at[2, p],
            )
        return crossing(
            far_crosses, i + 2, lambda: far_copy(p),
            gfar.at[p], g_relay.at[i], rnear.at[p], g_rsem.at[1, p],
        )

    own_sky = sky_ref[s]
    near_sky = [nb_ref[j, own_sky] for j in range(3)]

    def around(offset):
        sky = sky_ref[(s + sgn * offset + n) % n]
        here = (sky == near_sky[0]) | (sky == near_sky[1]) | (sky == near_sky[2])
        return here, vc_ref[sky]

    own_count = vc_ref[own_sky]
    has_far, far_count = around(-2)
    has_cross, cross_count = around(-1)
    _, sib_count = around(1)
    has_near, near_count = around(2)
    c0 = has_far
    c1 = has_far & has_cross
    c2 = jnp.logical_not(has_near)
    counts = (
        own_count,
        jnp.where(c0, far_count, cross_count),
        jnp.where(c1, cross_count, sib_count),
        jnp.where(c2, sib_count, near_count),
    )
    rows = lax.broadcasted_iota(jnp.int32, (BLK, PAIR), 0)
    for j in range(4):
        bias[j * BLK : (j + 1) * BLK, :] = jnp.where(rows < counts[j], 0.0, -jnp.inf).astype(F32)

    own_rows = pl.ds(pl.multiple_of(t * HALF, HALF), HALF)
    peer_rows = pl.ds(pl.multiple_of((1 - t) * HALF, HALF), HALF)

    loads[0].wait()
    loads[1].wait()
    acc[0] = dot(tok[...], wk[own_rows, :])
    loads[2].wait()
    acc[1] = dot(tok[...], wv[own_rows, :])
    loads[3].wait()
    acc[2] = dot(tok[...], wq[own_rows, :])
    tok_copy.wait_recv()
    for half in range(2):
        cols = slice(half * 256, half * 256 + 256)
        for j, w in ((0, wk), (1, wv)):
            value = (acc[j, :, cols] + dot(tokp[...], w[peer_rows, cols])).astype(BF16)
            kv_own[2 * half, j] = value[:, :PAIR]
            kv_own[2 * half + 1, j] = value[:, PAIR:]
        for p in (2 * half, 2 * half + 1):
            for o in (NEAR, FAR):
                if p in KV_RELAYED:
                    kv_crossing(o, KV_RELAYED.index(p)).start()
                else:
                    kv_copy(o, p).start()
            kv_copy(SIB, p).start()

    first = lax.broadcasted_iota(jnp.int32, (BLK, PAIR), 1) < 64

    def split(ref, value):
        for p in range(NP):
            part = value[:, p * PAIR : (p + 1) * PAIR]
            ref[p, :BLK, :] = jnp.where(first, part, 0.0).astype(BF16)
            ref[p, BLK:, :] = jnp.where(first, 0.0, part).astype(BF16)

    split(q2, (acc[2] + dot(tokp[...], wq[peer_rows, :])) * 0.125)
    for o in (NEAR, FAR):
        kv_crossing(o, 0).pass_on()
    loads[4].wait()
    loads[5].wait()
    acc[0] = dot_nt(go[...], wo[:, own_rows])
    go_copy.wait_recv()
    split(g2, acc[0] + dot_nt(gop[...], wo[:, peer_rows]))

    def forward_near(p):
        kv_copy(NEAR, p).wait_recv()
        kv_copy(CROSS, p).start()

    def combine_near(p):
        sib_copy(p).wait_recv()
        for j in range(2):
            gnear[p, j] = (near_g[p, j] + rsib[p, 1, j].astype(F32)).astype(BF16)

    def send_on(p, is_near):
        relayed = False
        for i, r in enumerate(G_RELAYED):
            pl.when(p == r)(lambda i=i: g_crossing(is_near, i).start())
            relayed = relayed | (p == r)

        @pl.when(jnp.logical_not(relayed))
        def _():
            (near_copy(p) if is_near else far_copy(p)).start()

    def pair_step(p):
        kv_copy(SIB, p).wait_recv()
        kv_copy(FAR, p).wait_recv()
        kv_copy(CROSS, p).wait_recv()
        for j, ref in ((0, kc), (1, vc)):
            ref[0:256, :] = kv_own[p, j]
            ref[256:512, :] = pick(c0, win[FAR, p, j], win[CROSS, p, j])
            ref[512:768, :] = pick(c1, win[CROSS, p, j], win[SIB, p, j])
            ref[768:1024, :] = pick(c2, win[SIB, p, j], win[NEAR, p, j])
        q = q2[p]
        g = g2[p]
        for k in range(4):
            ks = slice(k * BLK, (k + 1) * BLK)
            b = bias[ks, :]
            s_ref[ks, :] = dot_nt(kc[ks, :], q) + jnp.concatenate([b, b, b, b], axis=1)
            d_ref[ks, :] = dot_nt(vc[ks, :], g)
        for c in range(4):
            cols = slice(c * 128, (c + 1) * 128)
            top = jnp.max(s_ref[:, cols], axis=0, keepdims=True)
            total = jnp.zeros((8, 128), F32)
            mixed = jnp.zeros((8, 128), F32)
            for k in range(8):
                ks = slice(k * 128, (k + 1) * 128)
                e = jnp.exp(s_ref[ks, cols] - top)
                s_ref[ks, cols] = e
                total = total + jnp.sum(e.reshape(16, 8, 128), axis=0)
                mixed = mixed + jnp.sum((e * d_ref[ks, cols]).reshape(16, 8, 128), axis=0)
            inverse = 1.0 / jnp.sum(total, axis=0, keepdims=True)
            delta = jnp.sum(mixed, axis=0, keepdims=True) * inverse
            for k in range(8):
                ks = slice(k * 128, (k + 1) * 128)
                prob = s_ref[ks, cols] * inverse
                p_ref[ks, cols] = prob.astype(BF16)
                ds_ref[ks, cols] = (prob * (d_ref[ks, cols] - delta)).astype(BF16)

        def parts(j, left, right):
            def block(b):
                return dot(left[b * BLK : (b + 1) * BLK, :], right)

            own_g[p, j] = block(0)
            a, b, c = block(1), block(2), block(3)
            zero = jnp.zeros_like(a)
            gfar[p, j] = pick(c0, a, zero).astype(BF16)
            gsib[p, 1, j] = pick(c0, pick(c1, b, zero), a).astype(BF16)
            gsib[p, 0, j] = pick(c1, pick(c2, c, zero), b).astype(BF16)
            near_g[p, j] = pick(c2, zero, c)

        parts(0, ds_ref, q)
        parts(1, p_ref, g)
        sib_copy(p).start()
        send_on(p, False)
        lanes = pl.ds(pl.multiple_of(p * PAIR, PAIR), PAIR)
        for source, left, ref, scale in ((p_ref, vc, att, 1.0), (ds_ref, kc, dq, 0.125)):
            both = dot_tn(left[...], source[...])
            joined = jnp.concatenate([both[:64, :BLK], both[64:, BLK:]], axis=0) * scale
            ref[:, lanes] = joined.T.astype(BF16)

    forward_near(0)

    @pl.loop(0, NP)
    def _(p):
        @pl.when(p + 1 < NP)
        def _():
            forward_near(p + 1)

        @pl.when(p == 0)
        def _():
            for o in (NEAR, FAR):
                kv_crossing(o, 1).pass_on()

        pair_step(p)
        combine_near(p)
        send_on(p, True)
        for i in range(2):

            @pl.when(p == G_RELAYED[i] + 1)
            def _():
                for is_near in (True, False):
                    g_crossing(is_near, i).pass_on()

    osend[...] = dot(att[...], wo[:, peer_rows]).astype(BF16)
    out_copy.start()
    acc[0] = dot(att[...], wo[:, own_rows])
    acc[1] = dot_nt(dq[...], wq[peer_rows, :])
    acc[2] = dot_nt(dq[...], wq[own_rows, :])

    for p in range(NP):
        far_copy(p).wait_recv()
        near_copy(p).wait_recv()
        lanes = slice(p * PAIR, (p + 1) * PAIR)
        for j, ref in ((0, dk), (1, dv)):
            summed = own_g[p, j] + rsib[p, 0, j].astype(F32)
            summed = summed + rnear[p, j].astype(F32) + rfar[p, j].astype(F32)
            ref[:, lanes] = summed.astype(BF16)
    isend[...] = (
        acc[1] + dot_nt(dk[...], wk[peer_rows, :]) + dot_nt(dv[...], wv[peer_rows, :])
    ).astype(BF16)
    in_copy.start()
    out_copy.wait_recv()
    out_ref[...] = (acc[0] + orecv[...].astype(F32)).astype(BF16)
    acc[1] = acc[2] + dot_nt(dk[...], wk[own_rows, :]) + dot_nt(dv[...], wv[own_rows, :])
    in_copy.wait_recv()
    ig_ref[...] = (acc[1] + irecv[...].astype(F32)).astype(BF16)

    for copy in (tok_copy, go_copy, out_copy, in_copy):
        copy.wait_send()
    for p in range(NP):
        for o in range(4):
            if p in KV_RELAYED and o in (NEAR, FAR):
                kv_crossing(o, KV_RELAYED.index(p)).wait_send()
            else:
                kv_copy(o, p).wait_send()
        sib_copy(p).wait_send()
        for is_near in (True, False):
            if p in G_RELAYED:
                g_crossing(is_near, G_RELAYED.index(p)).wait_send()
            else:
                (near_copy(p) if is_near else far_copy(p)).wait_send()


def body(n, *args):
    args = args[:7] + (args[7].T,) + args[8:]
    wide = (BLK, HALF)
    half = pltpu.VMEM(wide, BF16)
    weight = pltpu.VMEM((2 * HALF, HALF), BF16)
    pair_kv = pltpu.VMEM((NP, 2, BLK, PAIR), BF16)
    pair_f32 = pltpu.VMEM((NP, 2, BLK, PAIR), F32)
    sib_kv = pltpu.VMEM((NP, 2, 2, BLK, PAIR), BF16)
    scratch = [
        half, half, half, half, weight, weight, weight, pltpu.VMEM((HALF, 2 * HALF), BF16),
        pltpu.VMEM((3,) + wide, F32),
        pair_kv, pltpu.VMEM((4, NP, 2, BLK, PAIR), BF16),
        pltpu.VMEM((NP, 2 * BLK, PAIR), BF16), pltpu.VMEM((NP, 2 * BLK, PAIR), BF16),
        pltpu.VMEM((4 * BLK, PAIR), F32),
        pltpu.VMEM((4 * BLK, PAIR), BF16), pltpu.VMEM((4 * BLK, PAIR), BF16),
        pltpu.VMEM((4 * BLK, 2 * BLK), F32), pltpu.VMEM((4 * BLK, 2 * BLK), F32),
        pltpu.VMEM((4 * BLK, 2 * BLK), BF16), pltpu.VMEM((4 * BLK, 2 * BLK), BF16),
        half, half, pair_f32, pair_f32, sib_kv, pair_kv, pair_kv, sib_kv, pair_kv, pair_kv, half, half,
        half, half, half, half,
        pltpu.VMEM((2, 2, BLK, PAIR), BF16), pltpu.VMEM((2, 2, BLK, PAIR), BF16),
        pltpu.SemaphoreType.DMA((8,)), pltpu.SemaphoreType.DMA((4,)),
        pltpu.SemaphoreType.DMA((6,)),
        pltpu.SemaphoreType.DMA((4,)), pltpu.SemaphoreType.DMA((4,)),
        pltpu.SemaphoreType.DMA((4, NP)), pltpu.SemaphoreType.DMA((4, NP)),
        pltpu.SemaphoreType.DMA((3, NP)), pltpu.SemaphoreType.DMA((3, NP)),
    ]
    shape = jax.ShapeDtypeStruct(wide, BF16)
    return pl.pallas_call(
        functools.partial(kernel, n),
        name="sky_attention",
        out_shape=(shape, shape),
        in_specs=[pl.BlockSpec(memory_space=pltpu.HBM)] * 6 + [pl.BlockSpec(memory_space=pltpu.SMEM)] * 3,
        out_specs=[pl.BlockSpec(memory_space=pltpu.VMEM)] * 2,
        scratch_shapes=scratch,
        compiler_params=pltpu.CompilerParams(
            collective_id=0, has_side_effects=True, vmem_limit_bytes=60 << 20
        ),
    )(*args)


def solution(mesh):
    placed = (
        P("seq", "tp"),
        P(None, "tp"),
        P(None, "tp"),
        P(None, "tp"),
        P("tp", None),
        P("seq", "tp"),
        P(),
        P(),
        P(),
    )
    return jax.shard_map(
        functools.partial(body, mesh.shape["seq"]),
        mesh=mesh,
        in_specs=placed,
        out_specs=(P("seq", "tp"), P("seq", "tp")),
        check_vma=False,
    )
```

```python
import functools

import jax
import jax.numpy as jnp
from jax import lax
from jax.experimental import pallas as pl
from jax.experimental.pallas import tpu as pltpu
from jax.sharding import PartitionSpec as P

MESH = pl.DeviceIdType.MESH
BLK = 256
PAIR = 128
NP = 4
HALF = 512
F32 = jnp.float32
BF16 = jnp.bfloat16

SIB, NEAR, FAR, CROSS = 0, 1, 2, 3


def dot(a, b):
    return jnp.dot(a, b, preferred_element_type=F32)


def dot_nt(a, b):
    return lax.dot_general(a, b, (((1,), (1,)), ((), ())), preferred_element_type=F32)


def dot_tn(a, b):
    return lax.dot_general(a, b, (((0,), (0,)), ((), ())), preferred_element_type=F32)


def pick(cond, a, b):
    return lax.select_n(cond, b, a)


def kernel(
    n,
    tok_hbm, wq_hbm, wk_hbm, wv_hbm, wo_hbm, go_hbm, sky_ref, nb_ref, vc_ref,
    out_ref, ig_ref,
    tok, tokp, go, gop, wq, wk, wv, wo, acc,
    kv_own, win, q2, g2, bias, kc, vc, s_ref, d_ref, p_ref, ds_ref,
    att, dq, own_g, near_g, gsib, gfar, gnear, rsib, rnear, rfar, dk, dv,
    osend, orecv, isend, irecv,
    lsem, tp_ssem, tp_rsem, kv_ssem, kv_rsem, g_ssem, g_rsem,
):
    s = lax.axis_index("seq")
    t = lax.axis_index("tp")
    sgn = 1 - 2 * (s % 2)

    def dev(offset):
        return ((s + sgn * offset + n) % n, t)

    sib, near, far, peer = dev(1), dev(2), dev(-2), (s, 1 - t)

    half_n = n // 2
    right_end = s % half_n >= half_n - 2
    left_end = s % half_n < 2
    even = s % 2 == 0
    near_crosses = (even & right_end) | (jnp.logical_not(even) & left_end)
    far_crosses = (even & left_end) | (jnp.logical_not(even) & right_end)

    def remote(src, dst, ssem, rsem, to):
        return pltpu.make_async_remote_copy(
            src_ref=src, dst_ref=dst, send_sem=ssem, recv_sem=rsem, device_id=to, device_id_type=MESH
        )

    def local(i, src, dst):
        return pltpu.make_async_copy(src, dst, lsem.at[i])

    loads = [
        local(0, tok_hbm, tok),
        local(1, wk_hbm, wk),
        local(2, wv_hbm, wv),
        local(3, wq_hbm, wq),
        local(4, go_hbm, go),
        local(5, wo_hbm, wo),
    ]
    for copy in loads:
        copy.start()

    barrier = pltpu.get_barrier_semaphore()
    for to in (peer, sib, near, far):
        pl.semaphore_signal(barrier, inc=1, device_id=to, device_id_type=MESH)
    pl.semaphore_wait(barrier, 4)

    def tp_copy(i, src, dst):
        return remote(src, dst, tp_ssem.at[i], tp_rsem.at[i], peer)

    tok_copy = tp_copy(0, tok_hbm, tokp)
    go_copy = tp_copy(1, go_hbm, gop)
    out_copy = tp_copy(2, osend, orecv)
    in_copy = tp_copy(3, isend, irecv)
    tok_copy.start()
    go_copy.start()

    def kv_copy(o, p):
        src = win.at[NEAR, p] if o == CROSS else kv_own.at[p]
        to = {SIB: sib, NEAR: far, FAR: near, CROSS: sib}[o]
        return remote(src, win.at[o, p], kv_ssem.at[o, p], kv_rsem.at[o, p], to)

    def sib_copy(p):
        return remote(gsib.at[p], rsib.at[p], g_ssem.at[0, p], g_rsem.at[0, p], sib)

    def far_copy(p):
        return remote(gfar.at[p], rnear.at[p], g_ssem.at[1, p], g_rsem.at[1, p], far)

    def near_copy(p):
        return remote(gnear.at[p], rfar.at[p], g_ssem.at[2, p], g_rsem.at[2, p], near)

    own_sky = sky_ref[s]
    near_sky = [nb_ref[j, own_sky] for j in range(3)]

    def around(offset):
        sky = sky_ref[(s + sgn * offset + n) % n]
        here = (sky == near_sky[0]) | (sky == near_sky[1]) | (sky == near_sky[2])
        return here, vc_ref[sky]

    own_count = vc_ref[own_sky]
    has_far, far_count = around(-2)
    has_cross, cross_count = around(-1)
    _, sib_count = around(1)
    has_near, near_count = around(2)
    c0 = has_far
    c1 = has_far & has_cross
    c2 = jnp.logical_not(has_near)
    counts = (
        own_count,
        jnp.where(c0, far_count, cross_count),
        jnp.where(c1, cross_count, sib_count),
        jnp.where(c2, sib_count, near_count),
    )
    rows = lax.broadcasted_iota(jnp.int32, (BLK, PAIR), 0)
    for j in range(4):
        bias[j * BLK : (j + 1) * BLK, :] = jnp.where(rows < counts[j], 0.0, -jnp.inf).astype(F32)

    own_rows = pl.ds(pl.multiple_of(t * HALF, HALF), HALF)
    peer_rows = pl.ds(pl.multiple_of((1 - t) * HALF, HALF), HALF)

    loads[0].wait()
    loads[1].wait()
    acc[0] = dot(tok[...], wk[own_rows, :])
    loads[2].wait()
    acc[1] = dot(tok[...], wv[own_rows, :])
    loads[3].wait()
    acc[2] = dot(tok[...], wq[own_rows, :])
    tok_copy.wait_recv()
    for half in range(2):
        cols = slice(half * 256, half * 256 + 256)
        for j, w in ((0, wk), (1, wv)):
            value = (acc[j, :, cols] + dot(tokp[...], w[peer_rows, cols])).astype(BF16)
            kv_own[2 * half, j] = value[:, :PAIR]
            kv_own[2 * half + 1, j] = value[:, PAIR:]
        for p in (2 * half, 2 * half + 1):
            for o, crosses in ((NEAR, far_crosses), (FAR, near_crosses)):
                pl.when(jnp.logical_not(crosses))(lambda o=o, p=p: kv_copy(o, p).start())
            kv_copy(SIB, p).start()

    first = lax.broadcasted_iota(jnp.int32, (BLK, PAIR), 1) < 64

    def split(ref, value):
        for p in range(NP):
            part = value[:, p * PAIR : (p + 1) * PAIR]
            ref[p, :BLK, :] = jnp.where(first, part, 0.0).astype(BF16)
            ref[p, BLK:, :] = jnp.where(first, 0.0, part).astype(BF16)

    split(q2, (acc[2] + dot(tokp[...], wq[peer_rows, :])) * 0.125)
    loads[4].wait()
    loads[5].wait()
    acc[0] = dot_nt(go[...], wo[:, own_rows])
    go_copy.wait_recv()

    for o, crosses in ((NEAR, far_crosses), (FAR, near_crosses)):

        @pl.when(crosses)
        def _():
            for p in range(NP):
                kv_copy(o, p).start()

    split(g2, acc[0] + dot_nt(gop[...], wo[:, peer_rows]))

    def forward_near(p):
        kv_copy(NEAR, p).wait_recv()
        kv_copy(CROSS, p).start()

    def combine_near(p):
        sib_copy(p).wait_recv()
        for j in range(2):
            gnear[p, j] = (near_g[p, j] + rsib[p, 1, j].astype(F32)).astype(BF16)

    def pair_step(p):
        kv_copy(SIB, p).wait_recv()
        kv_copy(FAR, p).wait_recv()
        kv_copy(CROSS, p).wait_recv()
        for j, ref in ((0, kc), (1, vc)):
            ref[0:256, :] = kv_own[p, j]
            ref[256:512, :] = pick(c0, win[FAR, p, j], win[CROSS, p, j])
            ref[512:768, :] = pick(c1, win[CROSS, p, j], win[SIB, p, j])
            ref[768:1024, :] = pick(c2, win[SIB, p, j], win[NEAR, p, j])
        q = q2[p]
        g = g2[p]
        for k in range(4):
            ks = slice(k * BLK, (k + 1) * BLK)
            b = bias[ks, :]
            s_ref[ks, :] = dot_nt(kc[ks, :], q) + jnp.concatenate([b, b, b, b], axis=1)
            d_ref[ks, :] = dot_nt(vc[ks, :], g)
        for c in range(4):
            cols = slice(c * 128, (c + 1) * 128)
            top = jnp.max(s_ref[:, cols], axis=0, keepdims=True)
            total = jnp.zeros((8, 128), F32)
            mixed = jnp.zeros((8, 128), F32)
            for k in range(8):
                ks = slice(k * 128, (k + 1) * 128)
                e = jnp.exp(s_ref[ks, cols] - top)
                s_ref[ks, cols] = e
                total = total + jnp.sum(e.reshape(16, 8, 128), axis=0)
                mixed = mixed + jnp.sum((e * d_ref[ks, cols]).reshape(16, 8, 128), axis=0)
            inverse = 1.0 / jnp.sum(total, axis=0, keepdims=True)
            delta = jnp.sum(mixed, axis=0, keepdims=True) * inverse
            for k in range(8):
                ks = slice(k * 128, (k + 1) * 128)
                prob = s_ref[ks, cols] * inverse
                p_ref[ks, cols] = prob.astype(BF16)
                ds_ref[ks, cols] = (prob * (d_ref[ks, cols] - delta)).astype(BF16)

        def parts(j, left, right):
            def block(b):
                return dot(left[b * BLK : (b + 1) * BLK, :], right)

            own_g[p, j] = block(0)
            a, b, c = block(1), block(2), block(3)
            zero = jnp.zeros_like(a)
            gfar[p, j] = pick(c0, a, zero).astype(BF16)
            gsib[p, 1, j] = pick(c0, pick(c1, b, zero), a).astype(BF16)
            gsib[p, 0, j] = pick(c1, pick(c2, c, zero), b).astype(BF16)
            near_g[p, j] = pick(c2, zero, c)

        between(p)
        parts(0, ds_ref, q)
        parts(1, p_ref, g)
        sib_copy(p).start()
        far_copy(p).start()
        lanes = pl.ds(pl.multiple_of(p * PAIR, PAIR), PAIR)
        for source, left, ref, scale in ((p_ref, vc, att, 1.0), (ds_ref, kc, dq, 0.125)):
            both = dot_tn(left[...], source[...])
            joined = jnp.concatenate([both[:64, :BLK], both[64:, BLK:]], axis=0) * scale
            ref[:, lanes] = joined.T.astype(BF16)

    forward_near(0)

    def finish(p):
        combine_near(p)
        near_copy(p).start()

    def between(p):
        @pl.when(p + 1 < NP)
        def _():
            forward_near(p + 1)

        @pl.when(p > 0)
        def _():
            finish(p - 1)

    @pl.loop(0, NP)
    def _(p):
        pair_step(p)

    finish(NP - 1)

    osend[...] = dot(att[...], wo[:, peer_rows]).astype(BF16)
    out_copy.start()
    acc[0] = dot(att[...], wo[:, own_rows])
    acc[1] = dot_nt(dq[...], wq[peer_rows, :])
    acc[2] = dot_nt(dq[...], wq[own_rows, :])

    for p in range(NP):
        far_copy(p).wait_recv()
        near_copy(p).wait_recv()
        lanes = slice(p * PAIR, (p + 1) * PAIR)
        for j, ref in ((0, dk), (1, dv)):
            summed = own_g[p, j] + rsib[p, 0, j].astype(F32)
            summed = summed + rnear[p, j].astype(F32) + rfar[p, j].astype(F32)
            ref[:, lanes] = summed.astype(BF16)
    isend[...] = (
        acc[1] + dot_nt(dk[...], wk[peer_rows, :]) + dot_nt(dv[...], wv[peer_rows, :])
    ).astype(BF16)
    in_copy.start()
    out_copy.wait_recv()
    out_ref[...] = (acc[0] + orecv[...].astype(F32)).astype(BF16)
    acc[1] = acc[2] + dot_nt(dk[...], wk[own_rows, :]) + dot_nt(dv[...], wv[own_rows, :])
    in_copy.wait_recv()
    ig_ref[...] = (acc[1] + irecv[...].astype(F32)).astype(BF16)

    for copy in (tok_copy, go_copy, out_copy, in_copy):
        copy.wait_send()
    for p in range(NP):
        for o in range(4):
            kv_copy(o, p).wait_send()
        for copy in (sib_copy(p), far_copy(p), near_copy(p)):
            copy.wait_send()


def body(n, *args):
    args = args[:7] + (args[7].T,) + args[8:]
    wide = (BLK, HALF)
    half = pltpu.VMEM(wide, BF16)
    weight = pltpu.VMEM((2 * HALF, HALF), BF16)
    pair_kv = pltpu.VMEM((NP, 2, BLK, PAIR), BF16)
    pair_f32 = pltpu.VMEM((NP, 2, BLK, PAIR), F32)
    sib_kv = pltpu.VMEM((NP, 2, 2, BLK, PAIR), BF16)
    scratch = [
        half, half, half, half, weight, weight, weight, pltpu.VMEM((HALF, 2 * HALF), BF16),
        pltpu.VMEM((3,) + wide, F32),
        pair_kv, pltpu.VMEM((4, NP, 2, BLK, PAIR), BF16),
        pltpu.VMEM((NP, 2 * BLK, PAIR), BF16), pltpu.VMEM((NP, 2 * BLK, PAIR), BF16),
        pltpu.VMEM((4 * BLK, PAIR), F32),
        pltpu.VMEM((4 * BLK, PAIR), BF16), pltpu.VMEM((4 * BLK, PAIR), BF16),
        pltpu.VMEM((4 * BLK, 2 * BLK), F32), pltpu.VMEM((4 * BLK, 2 * BLK), F32),
        pltpu.VMEM((4 * BLK, 2 * BLK), BF16), pltpu.VMEM((4 * BLK, 2 * BLK), BF16),
        half, half, pair_f32, pair_f32, sib_kv, pair_kv, pair_kv, sib_kv, pair_kv, pair_kv, half, half,
        half, half, half, half,
        pltpu.SemaphoreType.DMA((6,)),
        pltpu.SemaphoreType.DMA((4,)), pltpu.SemaphoreType.DMA((4,)),
        pltpu.SemaphoreType.DMA((4, NP)), pltpu.SemaphoreType.DMA((4, NP)),
        pltpu.SemaphoreType.DMA((3, NP)), pltpu.SemaphoreType.DMA((3, NP)),
    ]
    shape = jax.ShapeDtypeStruct(wide, BF16)
    return pl.pallas_call(
        functools.partial(kernel, n),
        name="sky_attention",
        out_shape=(shape, shape),
        in_specs=[pl.BlockSpec(memory_space=pltpu.HBM)] * 6 + [pl.BlockSpec(memory_space=pltpu.SMEM)] * 3,
        out_specs=[pl.BlockSpec(memory_space=pltpu.VMEM)] * 2,
        scratch_shapes=scratch,
        compiler_params=pltpu.CompilerParams(
            collective_id=0, has_side_effects=True, vmem_limit_bytes=60 << 20
        ),
    )(*args)


def solution(mesh):
    placed = (
        P("seq", "tp"),
        P(None, "tp"),
        P(None, "tp"),
        P(None, "tp"),
        P("tp", None),
        P("seq", "tp"),
        P(),
        P(),
        P(),
    )
    return jax.shard_map(
        functools.partial(body, mesh.shape["seq"]),
        mesh=mesh,
        in_specs=placed,
        out_specs=(P("seq", "tp"), P("seq", "tp")),
        check_vma=False,
    )
```

```python
import functools

import jax
import jax.numpy as jnp
from jax import lax
from jax.experimental import pallas as pl
from jax.experimental.pallas import tpu as pltpu
from jax.sharding import PartitionSpec as P

MESH = pl.DeviceIdType.MESH
BLK = 256
PAIR = 128
NP = 4
HALF = 512
F32 = jnp.float32
BF16 = jnp.bfloat16

SIB, NEAR, FAR, CROSS = 0, 1, 2, 3


def dot(a, b):
    return jnp.dot(a, b, preferred_element_type=F32)


def dot_nt(a, b):
    return lax.dot_general(a, b, (((1,), (1,)), ((), ())), preferred_element_type=F32)


def dot_tn(a, b):
    return lax.dot_general(a, b, (((0,), (0,)), ((), ())), preferred_element_type=F32)


def pick(cond, a, b):
    return lax.select_n(cond, b, a)


def kernel(
    n,
    tok_hbm, wq_hbm, wk_hbm, wv_hbm, wo_hbm, go_hbm, sky_ref, nb_ref, vc_ref,
    out_ref, ig_ref,
    tok, tokp, go, gop, wq, wk, wv, wo, acc,
    kv_own, win, q2, g2, bias, kc, vc, s_ref, d_ref, p_ref, ds_ref,
    att, dq, own_g, near_g, gsib, gfar, gnear, rsib, rnear, rfar, dk, dv,
    osend, orecv, isend, irecv,
    lsem, tp_ssem, tp_rsem, kv_ssem, kv_rsem, g_ssem, g_rsem,
):
    s = lax.axis_index("seq")
    t = lax.axis_index("tp")
    sgn = 1 - 2 * (s % 2)

    def dev(offset):
        return ((s + sgn * offset + n) % n, t)

    sib, near, far, peer = dev(1), dev(2), dev(-2), (s, 1 - t)

    half_n = n // 2
    right_end = s % half_n >= half_n - 2
    left_end = s % half_n < 2
    even = s % 2 == 0
    near_crosses = (even & right_end) | (jnp.logical_not(even) & left_end)
    far_crosses = (even & left_end) | (jnp.logical_not(even) & right_end)

    def remote(src, dst, ssem, rsem, to):
        return pltpu.make_async_remote_copy(
            src_ref=src, dst_ref=dst, send_sem=ssem, recv_sem=rsem, device_id=to, device_id_type=MESH
        )

    def local(i, src, dst):
        return pltpu.make_async_copy(src, dst, lsem.at[i])

    loads = [
        local(0, tok_hbm, tok),
        local(1, wk_hbm, wk),
        local(2, wv_hbm, wv),
        local(3, wq_hbm, wq),
        local(4, go_hbm, go),
        local(5, wo_hbm, wo),
    ]
    for copy in loads:
        copy.start()

    barrier = pltpu.get_barrier_semaphore()
    for to in (peer, sib, near, far):
        pl.semaphore_signal(barrier, inc=1, device_id=to, device_id_type=MESH)
    pl.semaphore_wait(barrier, 4)

    def tp_copy(i, src, dst):
        return remote(src, dst, tp_ssem.at[i], tp_rsem.at[i], peer)

    tok_copy = tp_copy(0, tok_hbm, tokp)
    go_copy = tp_copy(1, go_hbm, gop)
    out_copy = tp_copy(2, osend, orecv)
    in_copy = tp_copy(3, isend, irecv)
    tok_copy.start()
    go_copy.start()

    def kv_copy(o, p):
        src = win.at[NEAR, p] if o == CROSS else kv_own.at[p]
        to = {SIB: sib, NEAR: far, FAR: near, CROSS: sib}[o]
        return remote(src, win.at[o, p], kv_ssem.at[o, p], kv_rsem.at[o, p], to)

    def sib_copy(p):
        return remote(gsib.at[p], rsib.at[p], g_ssem.at[0, p], g_rsem.at[0, p], sib)

    def far_copy(p):
        return remote(gfar.at[p], rnear.at[p], g_ssem.at[1, p], g_rsem.at[1, p], far)

    def near_copy(p):
        return remote(gnear.at[p], rfar.at[p], g_ssem.at[2, p], g_rsem.at[2, p], near)

    own_sky = sky_ref[s]
    near_sky = [nb_ref[j, own_sky] for j in range(3)]

    def around(offset):
        sky = sky_ref[(s + sgn * offset + n) % n]
        here = (sky == near_sky[0]) | (sky == near_sky[1]) | (sky == near_sky[2])
        return here, vc_ref[sky]

    own_count = vc_ref[own_sky]
    has_far, far_count = around(-2)
    has_cross, cross_count = around(-1)
    _, sib_count = around(1)
    has_near, near_count = around(2)
    c0 = has_far
    c1 = has_far & has_cross
    c2 = jnp.logical_not(has_near)
    counts = (
        own_count,
        jnp.where(c0, far_count, cross_count),
        jnp.where(c1, cross_count, sib_count),
        jnp.where(c2, sib_count, near_count),
    )
    rows = lax.broadcasted_iota(jnp.int32, (BLK, PAIR), 0)
    for j in range(4):
        bias[j * BLK : (j + 1) * BLK, :] = jnp.where(rows < counts[j], 0.0, -jnp.inf).astype(F32)

    own_rows = pl.ds(pl.multiple_of(t * HALF, HALF), HALF)
    peer_rows = pl.ds(pl.multiple_of((1 - t) * HALF, HALF), HALF)

    loads[0].wait()
    loads[1].wait()
    acc[0] = dot(tok[...], wk[own_rows, :])
    loads[2].wait()
    acc[1] = dot(tok[...], wv[own_rows, :])
    loads[3].wait()
    acc[2] = dot(tok[...], wq[own_rows, :])
    tok_copy.wait_recv()
    for half in range(2):
        cols = slice(half * 256, half * 256 + 256)
        for j, w in ((0, wk), (1, wv)):
            value = (acc[j, :, cols] + dot(tokp[...], w[peer_rows, cols])).astype(BF16)
            kv_own[2 * half, j] = value[:, :PAIR]
            kv_own[2 * half + 1, j] = value[:, PAIR:]
        for p in (2 * half, 2 * half + 1):
            for o, crosses in ((NEAR, far_crosses), (FAR, near_crosses)):
                pl.when(jnp.logical_not(crosses))(lambda o=o, p=p: kv_copy(o, p).start())
            kv_copy(SIB, p).start()

    first = lax.broadcasted_iota(jnp.int32, (BLK, PAIR), 1) < 64

    def split(ref, value):
        for p in range(NP):
            part = value[:, p * PAIR : (p + 1) * PAIR]
            ref[p, :BLK, :] = jnp.where(first, part, 0.0).astype(BF16)
            ref[p, BLK:, :] = jnp.where(first, 0.0, part).astype(BF16)

    split(q2, (acc[2] + dot(tokp[...], wq[peer_rows, :])) * 0.125)
    loads[4].wait()
    loads[5].wait()
    acc[0] = dot_nt(go[...], wo[:, own_rows])
    go_copy.wait_recv()

    for o, crosses in ((NEAR, far_crosses), (FAR, near_crosses)):

        @pl.when(crosses)
        def _():
            for p in range(NP):
                kv_copy(o, p).start()

    split(g2, acc[0] + dot_nt(gop[...], wo[:, peer_rows]))

    def forward_near(p):
        kv_copy(NEAR, p).wait_recv()
        kv_copy(CROSS, p).start()

    def combine_near(p):
        sib_copy(p).wait_recv()
        for j in range(2):
            gnear[p, j] = (near_g[p, j] + rsib[p, 1, j].astype(F32)).astype(BF16)

    def pair_step(p):
        kv_copy(SIB, p).wait_recv()
        kv_copy(FAR, p).wait_recv()
        kv_copy(CROSS, p).wait_recv()
        for j, ref in ((0, kc), (1, vc)):
            ref[0:256, :] = kv_own[p, j]
            ref[256:512, :] = pick(c0, win[FAR, p, j], win[CROSS, p, j])
            ref[512:768, :] = pick(c1, win[CROSS, p, j], win[SIB, p, j])
            ref[768:1024, :] = pick(c2, win[SIB, p, j], win[NEAR, p, j])
        q = q2[p]
        g = g2[p]
        for k in range(4):
            ks = slice(k * BLK, (k + 1) * BLK)
            b = bias[ks, :]
            s_ref[ks, :] = dot_nt(kc[ks, :], q) + jnp.concatenate([b, b, b, b], axis=1)
            d_ref[ks, :] = dot_nt(vc[ks, :], g)
        for c in range(4):
            cols = slice(c * 128, (c + 1) * 128)
            top = jnp.max(s_ref[:, cols], axis=0, keepdims=True)
            total = jnp.zeros((8, 128), F32)
            mixed = jnp.zeros((8, 128), F32)
            for k in range(8):
                ks = slice(k * 128, (k + 1) * 128)
                e = jnp.exp(s_ref[ks, cols] - top)
                s_ref[ks, cols] = e
                total = total + jnp.sum(e.reshape(16, 8, 128), axis=0)
                mixed = mixed + jnp.sum((e * d_ref[ks, cols]).reshape(16, 8, 128), axis=0)
            inverse = 1.0 / jnp.sum(total, axis=0, keepdims=True)
            delta = jnp.sum(mixed, axis=0, keepdims=True) * inverse
            for k in range(8):
                ks = slice(k * 128, (k + 1) * 128)
                prob = s_ref[ks, cols] * inverse
                p_ref[ks, cols] = prob.astype(BF16)
                ds_ref[ks, cols] = (prob * (d_ref[ks, cols] - delta)).astype(BF16)

        def parts(j, left, right):
            def block(b):
                return dot(left[b * BLK : (b + 1) * BLK, :], right)

            own_g[p, j] = block(0)
            a, b, c = block(1), block(2), block(3)
            zero = jnp.zeros_like(a)
            gfar[p, j] = pick(c0, a, zero).astype(BF16)
            gsib[p, 1, j] = pick(c0, pick(c1, b, zero), a).astype(BF16)
            gsib[p, 0, j] = pick(c1, pick(c2, c, zero), b).astype(BF16)
            near_g[p, j] = pick(c2, zero, c)

        between(p)
        parts(0, ds_ref, q)
        parts(1, p_ref, g)
        sib_copy(p).start()
        far_copy(p).start()
        lanes = pl.ds(pl.multiple_of(p * PAIR, PAIR), PAIR)
        for source, left, ref, scale in ((p_ref, vc, att, 1.0), (ds_ref, kc, dq, 0.125)):
            both = dot_tn(left[...], source[...])
            joined = jnp.concatenate([both[:64, :BLK], both[64:, BLK:]], axis=0) * scale
            ref[:, lanes] = joined.T.astype(BF16)

    forward_near(0)

    def finish(p):
        combine_near(p)
        near_copy(p).start()

    def between(p):
        @pl.when(p + 1 < NP)
        def _():
            forward_near(p + 1)

        @pl.when(p > 0)
        def _():
            finish(p - 1)

    @pl.loop(0, NP)
    def _(p):
        pair_step(p)

    finish(NP - 1)

    osend[...] = dot(att[...], wo[:, peer_rows]).astype(BF16)
    out_copy.start()
    acc[0] = dot(att[...], wo[:, own_rows])
    acc[1] = dot_nt(dq[...], wq[peer_rows, :])
    acc[2] = dot_nt(dq[...], wq[own_rows, :])

    for p in range(NP):
        far_copy(p).wait_recv()
        near_copy(p).wait_recv()
        lanes = slice(p * PAIR, (p + 1) * PAIR)
        for j, ref in ((0, dk), (1, dv)):
            summed = own_g[p, j] + rsib[p, 0, j].astype(F32)
            summed = summed + rnear[p, j].astype(F32) + rfar[p, j].astype(F32)
            ref[:, lanes] = summed.astype(BF16)
    isend[...] = (
        acc[1] + dot_nt(dk[...], wk[peer_rows, :]) + dot_nt(dv[...], wv[peer_rows, :])
    ).astype(BF16)
    in_copy.start()
    out_copy.wait_recv()
    out_ref[...] = (acc[0] + orecv[...].astype(F32)).astype(BF16)
    acc[1] = acc[2] + dot_nt(dk[...], wk[own_rows, :]) + dot_nt(dv[...], wv[own_rows, :])
    in_copy.wait_recv()
    ig_ref[...] = (acc[1] + irecv[...].astype(F32)).astype(BF16)

    for copy in (tok_copy, go_copy, out_copy, in_copy):
        copy.wait_send()
    for p in range(NP):
        for o in range(4):
            kv_copy(o, p).wait_send()
        for copy in (sib_copy(p), far_copy(p), near_copy(p)):
            copy.wait_send()


def body(n, *args):
    args = args[:7] + (args[7].T,) + args[8:]
    wide = (BLK, HALF)
    half = pltpu.VMEM(wide, BF16)
    weight = pltpu.VMEM((2 * HALF, HALF), BF16)
    pair_kv = pltpu.VMEM((NP, 2, BLK, PAIR), BF16)
    pair_f32 = pltpu.VMEM((NP, 2, BLK, PAIR), F32)
    sib_kv = pltpu.VMEM((NP, 2, 2, BLK, PAIR), BF16)
    scratch = [
        half, half, half, half, weight, weight, weight, pltpu.VMEM((HALF, 2 * HALF), BF16),
        pltpu.VMEM((3,) + wide, F32),
        pair_kv, pltpu.VMEM((4, NP, 2, BLK, PAIR), BF16),
        pltpu.VMEM((NP, 2 * BLK, PAIR), BF16), pltpu.VMEM((NP, 2 * BLK, PAIR), BF16),
        pltpu.VMEM((4 * BLK, PAIR), F32),
        pltpu.VMEM((4 * BLK, PAIR), BF16), pltpu.VMEM((4 * BLK, PAIR), BF16),
        pltpu.VMEM((4 * BLK, 2 * BLK), F32), pltpu.VMEM((4 * BLK, 2 * BLK), F32),
        pltpu.VMEM((4 * BLK, 2 * BLK), BF16), pltpu.VMEM((4 * BLK, 2 * BLK), BF16),
        half, half, pair_f32, pair_f32, sib_kv, pair_kv, pair_kv, sib_kv, pair_kv, pair_kv, half, half,
        half, half, half, half,
        pltpu.SemaphoreType.DMA((6,)),
        pltpu.SemaphoreType.DMA((4,)), pltpu.SemaphoreType.DMA((4,)),
        pltpu.SemaphoreType.DMA((4, NP)), pltpu.SemaphoreType.DMA((4, NP)),
        pltpu.SemaphoreType.DMA((3, NP)), pltpu.SemaphoreType.DMA((3, NP)),
    ]
    shape = jax.ShapeDtypeStruct(wide, BF16)
    return pl.pallas_call(
        functools.partial(kernel, n),
        name="sky_attention",
        out_shape=(shape, shape),
        in_specs=[pl.BlockSpec(memory_space=pltpu.HBM)] * 6 + [pl.BlockSpec(memory_space=pltpu.SMEM)] * 3,
        out_specs=[pl.BlockSpec(memory_space=pltpu.VMEM)] * 2,
        scratch_shapes=scratch,
        compiler_params=pltpu.CompilerParams(
            collective_id=0, has_side_effects=True, vmem_limit_bytes=213 << 18
        ),
    )(*args)


def solution(mesh):
    placed = (
        P("seq", "tp"),
        P(None, "tp"),
        P(None, "tp"),
        P(None, "tp"),
        P("tp", None),
        P("seq", "tp"),
        P(),
        P(),
        P(),
    )
    return jax.shard_map(
        functools.partial(body, mesh.shape["seq"]),
        mesh=mesh,
        in_specs=placed,
        out_specs=(P("seq", "tp"), P("seq", "tp")),
        check_vma=False,
    )
```

```python
import functools

import jax
import jax.numpy as jnp
from jax import lax
from jax.experimental import pallas as pl
from jax.experimental.pallas import tpu as pltpu
from jax.sharding import PartitionSpec as P

MESH = pl.DeviceIdType.MESH
BLK = 256
PAIR = 128
NP = 4
HALF = 512
F32 = jnp.float32
BF16 = jnp.bfloat16

SIB, NEAR, FAR, CROSS = 0, 1, 2, 3


def dot(a, b):
    return jnp.dot(a, b, preferred_element_type=F32)


def dot_nt(a, b):
    return lax.dot_general(a, b, (((1,), (1,)), ((), ())), preferred_element_type=F32)


def dot_tn(a, b):
    return lax.dot_general(a, b, (((0,), (0,)), ((), ())), preferred_element_type=F32)


def pick(cond, a, b):
    return lax.select_n(cond, b, a)


def kernel(
    n,
    tok_hbm, wq_hbm, wk_hbm, wv_hbm, wo_hbm, go_hbm, sky_ref, nb_ref, vc_ref,
    out_ref, ig_ref,
    tok, tokp, go, gop, wq, wk, wv, wo, acc,
    kv_own, win, q2, g2, bias, kc, vc, s_ref, d_ref, p_ref, ds_ref,
    att, dq, own_g, near_g, gsib, gfar, gnear, rsib, rnear, rfar, dk, dv,
    osend, orecv, isend, irecv,
    lsem, tp_ssem, tp_rsem, kv_ssem, kv_rsem, g_ssem, g_rsem,
):
    s = lax.axis_index("seq")
    t = lax.axis_index("tp")
    sgn = 1 - 2 * (s % 2)

    def dev(offset):
        return ((s + sgn * offset + n) % n, t)

    sib, near, far, peer = dev(1), dev(2), dev(-2), (s, 1 - t)

    half_n = n // 2
    right_end = s % half_n >= half_n - 2
    left_end = s % half_n < 2
    even = s % 2 == 0
    near_crosses = (even & right_end) | (jnp.logical_not(even) & left_end)
    far_crosses = (even & left_end) | (jnp.logical_not(even) & right_end)

    def remote(src, dst, ssem, rsem, to):
        return pltpu.make_async_remote_copy(
            src_ref=src, dst_ref=dst, send_sem=ssem, recv_sem=rsem, device_id=to, device_id_type=MESH
        )

    def local(i, src, dst):
        return pltpu.make_async_copy(src, dst, lsem.at[i])

    loads = [
        local(0, tok_hbm, tok),
        local(1, wk_hbm, wk),
        local(2, wv_hbm, wv),
        local(3, wq_hbm, wq),
        local(4, go_hbm, go),
        local(5, wo_hbm, wo),
    ]
    for copy in loads:
        copy.start()

    barrier = pltpu.get_barrier_semaphore()
    for to in (peer, sib, near, far):
        pl.semaphore_signal(barrier, inc=1, device_id=to, device_id_type=MESH)
    pl.semaphore_wait(barrier, 4)

    def tp_copy(i, src, dst):
        return remote(src, dst, tp_ssem.at[i], tp_rsem.at[i], peer)

    tok_copy = tp_copy(0, tok_hbm, tokp)
    go_copy = tp_copy(1, go_hbm, gop)
    out_copy = tp_copy(2, osend, orecv)
    in_copy = tp_copy(3, isend, irecv)
    tok_copy.start()
    go_copy.start()

    def kv_copy(o, p):
        src = win.at[NEAR, p] if o == CROSS else kv_own.at[p]
        to = {SIB: sib, NEAR: far, FAR: near, CROSS: sib}[o]
        return remote(src, win.at[o, p], kv_ssem.at[o, p], kv_rsem.at[o, p], to)

    def sib_copy(p):
        return remote(gsib.at[p], rsib.at[p], g_ssem.at[0, p], g_rsem.at[0, p], sib)

    def far_copy(p):
        return remote(gfar.at[p], rnear.at[p], g_ssem.at[1, p], g_rsem.at[1, p], far)

    def near_copy(p):
        return remote(gnear.at[p], rfar.at[p], g_ssem.at[2, p], g_rsem.at[2, p], near)

    own_sky = sky_ref[s]
    near_sky = [nb_ref[j, own_sky] for j in range(3)]

    def around(offset):
        sky = sky_ref[(s + sgn * offset + n) % n]
        here = (sky == near_sky[0]) | (sky == near_sky[1]) | (sky == near_sky[2])
        return here, vc_ref[sky]

    own_count = vc_ref[own_sky]
    has_far, far_count = around(-2)
    has_cross, cross_count = around(-1)
    _, sib_count = around(1)
    has_near, near_count = around(2)
    c0 = has_far
    c1 = has_far & has_cross
    c2 = jnp.logical_not(has_near)
    counts = (
        own_count,
        jnp.where(c0, far_count, cross_count),
        jnp.where(c1, cross_count, sib_count),
        jnp.where(c2, sib_count, near_count),
    )
    rows = lax.broadcasted_iota(jnp.int32, (BLK, PAIR), 0)
    for j in range(4):
        bias[j * BLK : (j + 1) * BLK, :] = jnp.where(rows < counts[j], 0.0, -jnp.inf).astype(F32)

    own_rows = pl.ds(pl.multiple_of(t * HALF, HALF), HALF)
    peer_rows = pl.ds(pl.multiple_of((1 - t) * HALF, HALF), HALF)

    loads[0].wait()
    loads[1].wait()
    acc[0] = dot(tok[...], wk[own_rows, :])
    loads[2].wait()
    acc[1] = dot(tok[...], wv[own_rows, :])
    loads[3].wait()
    acc[2] = dot(tok[...], wq[own_rows, :])
    tok_copy.wait_recv()
    for half in range(2):
        cols = slice(half * 256, half * 256 + 256)
        for j, w in ((0, wk), (1, wv)):
            value = (acc[j, :, cols] + dot(tokp[...], w[peer_rows, cols])).astype(BF16)
            kv_own[2 * half, j] = value[:, :PAIR]
            kv_own[2 * half + 1, j] = value[:, PAIR:]
        for p in (2 * half, 2 * half + 1):
            for o, crosses in ((NEAR, far_crosses), (FAR, near_crosses)):
                pl.when(jnp.logical_not(crosses))(lambda o=o, p=p: kv_copy(o, p).start())
            kv_copy(SIB, p).start()

    first = lax.broadcasted_iota(jnp.int32, (BLK, PAIR), 1) < 64

    def split(ref, value):
        for p in range(NP):
            part = value[:, p * PAIR : (p + 1) * PAIR]
            ref[p, :BLK, :] = jnp.where(first, part, 0.0).astype(BF16)
            ref[p, BLK:, :] = jnp.where(first, 0.0, part).astype(BF16)

    split(q2, (acc[2] + dot(tokp[...], wq[peer_rows, :])) * 0.125)
    loads[4].wait()
    loads[5].wait()
    acc[0] = dot_nt(go[...], wo[:, own_rows])
    go_copy.wait_recv()

    for o, crosses in ((NEAR, far_crosses), (FAR, near_crosses)):

        @pl.when(crosses)
        def _():
            for p in range(NP):
                kv_copy(o, p).start()

    split(g2, acc[0] + dot_nt(gop[...], wo[:, peer_rows]))

    def forward_near(p):
        kv_copy(NEAR, p).wait_recv()
        kv_copy(CROSS, p).start()

    def combine_near(p):
        sib_copy(p).wait_recv()
        for j in range(2):
            gnear[p, j] = (near_g[p, j] + rsib[p, 1, j].astype(F32)).astype(BF16)

    def pair_step(p):
        kv_copy(SIB, p).wait_recv()
        kv_copy(FAR, p).wait_recv()
        kv_copy(CROSS, p).wait_recv()
        for j, ref in ((0, kc), (1, vc)):
            ref[0:256, :] = kv_own[p, j]
            ref[256:512, :] = pick(c0, win[FAR, p, j], win[CROSS, p, j])
            ref[512:768, :] = pick(c1, win[CROSS, p, j], win[SIB, p, j])
            ref[768:1024, :] = pick(c2, win[SIB, p, j], win[NEAR, p, j])
        q = q2[p]
        g = g2[p]
        for k in range(4):
            ks = slice(k * BLK, (k + 1) * BLK)
            b = bias[ks, :]
            s_ref[ks, :] = dot_nt(kc[ks, :], q) + jnp.concatenate([b, b, b, b], axis=1)
            d_ref[ks, :] = dot_nt(vc[ks, :], g)
        for c in range(4):
            cols = slice(c * 128, (c + 1) * 128)
            top = jnp.max(s_ref[:, cols], axis=0, keepdims=True)
            total = jnp.zeros((8, 128), F32)
            mixed = jnp.zeros((8, 128), F32)
            for k in range(8):
                ks = slice(k * 128, (k + 1) * 128)
                e = jnp.exp(s_ref[ks, cols] - top)
                s_ref[ks, cols] = e
                total = total + jnp.sum(e.reshape(16, 8, 128), axis=0)
                mixed = mixed + jnp.sum((e * d_ref[ks, cols]).reshape(16, 8, 128), axis=0)
            inverse = 1.0 / jnp.sum(total, axis=0, keepdims=True)
            delta = jnp.sum(mixed, axis=0, keepdims=True) * inverse
            for k in range(8):
                ks = slice(k * 128, (k + 1) * 128)
                prob = s_ref[ks, cols] * inverse
                p_ref[ks, cols] = prob.astype(BF16)
                ds_ref[ks, cols] = (prob * (d_ref[ks, cols] - delta)).astype(BF16)

        def parts(j, left, right):
            def block(b):
                return dot(left[b * BLK : (b + 1) * BLK, :], right)

            own_g[p, j] = block(0)
            a, b, c = block(1), block(2), block(3)
            zero = jnp.zeros_like(a)
            gfar[p, j] = pick(c0, a, zero).astype(BF16)
            gsib[p, 1, j] = pick(c0, pick(c1, b, zero), a).astype(BF16)
            gsib[p, 0, j] = pick(c1, pick(c2, c, zero), b).astype(BF16)
            near_g[p, j] = pick(c2, zero, c)

        between(p)
        parts(0, ds_ref, q)
        parts(1, p_ref, g)
        sib_copy(p).start()
        far_copy(p).start()
        lanes = pl.ds(pl.multiple_of(p * PAIR, PAIR), PAIR)
        for source, left, ref, scale in ((p_ref, vc, att, 1.0), (ds_ref, kc, dq, 0.125)):
            both = dot_tn(left[...], source[...])
            joined = jnp.concatenate([both[:64, :BLK], both[64:, BLK:]], axis=0) * scale
            ref[:, lanes] = joined.T.astype(BF16)

    forward_near(0)

    def finish(p):
        combine_near(p)
        near_copy(p).start()

    def between(p):
        @pl.when(p + 1 < NP)
        def _():
            forward_near(p + 1)

        @pl.when(p > 0)
        def _():
            finish(p - 1)

    @pl.loop(0, NP)
    def _(p):
        pair_step(p)

    finish(NP - 1)

    osend[...] = dot(att[...], wo[:, peer_rows]).astype(BF16)
    out_copy.start()
    acc[0] = dot(att[...], wo[:, own_rows])
    acc[1] = dot_nt(dq[...], wq[peer_rows, :])
    acc[2] = dot_nt(dq[...], wq[own_rows, :])

    for p in range(NP):
        far_copy(p).wait_recv()
        near_copy(p).wait_recv()
        lanes = slice(p * PAIR, (p + 1) * PAIR)
        for j, ref in ((0, dk), (1, dv)):
            summed = own_g[p, j] + rsib[p, 0, j].astype(F32)
            summed = summed + rnear[p, j].astype(F32) + rfar[p, j].astype(F32)
            ref[:, lanes] = summed.astype(BF16)
    isend[...] = (
        acc[1] + dot_nt(dk[...], wk[peer_rows, :]) + dot_nt(dv[...], wv[peer_rows, :])
    ).astype(BF16)
    in_copy.start()
    out_copy.wait_recv()
    out_ref[...] = (acc[0] + orecv[...].astype(F32)).astype(BF16)
    acc[1] = acc[2] + dot_nt(dk[...], wk[own_rows, :]) + dot_nt(dv[...], wv[own_rows, :])
    in_copy.wait_recv()
    ig_ref[...] = (acc[1] + irecv[...].astype(F32)).astype(BF16)

    for copy in (tok_copy, go_copy, out_copy, in_copy):
        copy.wait_send()
    for p in range(NP):
        for o in range(4):
            kv_copy(o, p).wait_send()
        for copy in (sib_copy(p), far_copy(p), near_copy(p)):
            copy.wait_send()


def body(n, *args):
    args = args[:7] + (args[7].T,) + args[8:]
    args = args[:6] + tuple(pltpu.with_memory_space_constraint(x, pltpu.HBM) for x in args[6:])
    wide = (BLK, HALF)
    half = pltpu.VMEM(wide, BF16)
    weight = pltpu.VMEM((2 * HALF, HALF), BF16)
    pair_kv = pltpu.VMEM((NP, 2, BLK, PAIR), BF16)
    pair_f32 = pltpu.VMEM((NP, 2, BLK, PAIR), F32)
    sib_kv = pltpu.VMEM((NP, 2, 2, BLK, PAIR), BF16)
    scratch = [
        half, half, half, half, weight, weight, weight, pltpu.VMEM((HALF, 2 * HALF), BF16),
        pltpu.VMEM((3,) + wide, F32),
        pair_kv, pltpu.VMEM((4, NP, 2, BLK, PAIR), BF16),
        pltpu.VMEM((NP, 2 * BLK, PAIR), BF16), pltpu.VMEM((NP, 2 * BLK, PAIR), BF16),
        pltpu.VMEM((4 * BLK, PAIR), F32),
        pltpu.VMEM((4 * BLK, PAIR), BF16), pltpu.VMEM((4 * BLK, PAIR), BF16),
        pltpu.VMEM((4 * BLK, 2 * BLK), F32), pltpu.VMEM((4 * BLK, 2 * BLK), F32),
        pltpu.VMEM((4 * BLK, 2 * BLK), BF16), pltpu.VMEM((4 * BLK, 2 * BLK), BF16),
        half, half, pair_f32, pair_f32, sib_kv, pair_kv, pair_kv, sib_kv, pair_kv, pair_kv, half, half,
        half, half, half, half,
        pltpu.SemaphoreType.DMA((6,)),
        pltpu.SemaphoreType.DMA((4,)), pltpu.SemaphoreType.DMA((4,)),
        pltpu.SemaphoreType.DMA((4, NP)), pltpu.SemaphoreType.DMA((4, NP)),
        pltpu.SemaphoreType.DMA((3, NP)), pltpu.SemaphoreType.DMA((3, NP)),
    ]
    shape = jax.ShapeDtypeStruct(wide, BF16)
    return pl.pallas_call(
        functools.partial(kernel, n),
        name="sky_attention",
        out_shape=(shape, shape),
        in_specs=[pl.BlockSpec(memory_space=pltpu.HBM)] * 6 + [pl.BlockSpec(memory_space=pltpu.SMEM)] * 3,
        out_specs=[pl.BlockSpec(memory_space=pltpu.VMEM)] * 2,
        scratch_shapes=scratch,
        compiler_params=pltpu.CompilerParams(
            collective_id=0, has_side_effects=True, vmem_limit_bytes=213 << 18
        ),
    )(*args)


def solution(mesh):
    placed = (
        P("seq", "tp"),
        P(None, "tp"),
        P(None, "tp"),
        P(None, "tp"),
        P("tp", None),
        P("seq", "tp"),
        P(),
        P(),
        P(),
    )
    return jax.shard_map(
        functools.partial(body, mesh.shape["seq"]),
        mesh=mesh,
        in_specs=placed,
        out_specs=(P("seq", "tp"), P("seq", "tp")),
        check_vma=False,
    )
```

```python
import functools

import jax
import jax.numpy as jnp
from jax import lax
from jax.experimental import pallas as pl
from jax.experimental.pallas import tpu as pltpu
from jax.sharding import PartitionSpec as P

MESH = pl.DeviceIdType.MESH
BLK = 256
PAIR = 128
NP = 4
HALF = 512
F32 = jnp.float32
BF16 = jnp.bfloat16

SIB, NEAR, FAR, CROSS = 0, 1, 2, 3


def dot(a, b):
    return jnp.dot(a, b, preferred_element_type=F32)


def dot_nt(a, b):
    return lax.dot_general(a, b, (((1,), (1,)), ((), ())), preferred_element_type=F32)


def dot_tn(a, b):
    return lax.dot_general(a, b, (((0,), (0,)), ((), ())), preferred_element_type=F32)


def pick(cond, a, b):
    return lax.select_n(cond, b, a)


def kernel(
    n,
    tok_hbm, wq_hbm, wk_hbm, wv_hbm, wo_hbm, go_hbm, sky_ref, nb_ref, vc_ref,
    out_ref, ig_ref,
    tok, tokp, go, gop, wq, wk, wv, wo, acc,
    kv_own, win, q2, g2, bias, kc, vc, s_ref, d_ref, p_ref, ds_ref,
    att, dq, own_g, near_g, gsib, gfar, gnear, rsib, rnear, rfar, dk, dv,
    osend, orecv, isend, irecv,
    lsem, tp_ssem, tp_rsem, kv_ssem, kv_rsem, g_ssem, g_rsem,
):
    s = lax.axis_index("seq")
    t = lax.axis_index("tp")
    sgn = 1 - 2 * (s % 2)

    def dev(offset):
        return ((s + sgn * offset + n) % n, t)

    sib, near, far, peer = dev(1), dev(2), dev(-2), (s, 1 - t)

    half_n = n // 2
    right_end = s % half_n >= half_n - 2
    left_end = s % half_n < 2
    even = s % 2 == 0
    near_crosses = (even & right_end) | (jnp.logical_not(even) & left_end)
    far_crosses = (even & left_end) | (jnp.logical_not(even) & right_end)

    def remote(src, dst, ssem, rsem, to):
        return pltpu.make_async_remote_copy(
            src_ref=src, dst_ref=dst, send_sem=ssem, recv_sem=rsem, device_id=to, device_id_type=MESH
        )

    def local(i, src, dst):
        return pltpu.make_async_copy(src, dst, lsem.at[i])

    loads = [
        local(0, tok_hbm, tok),
        local(1, wk_hbm, wk),
        local(2, wv_hbm, wv),
        local(3, wq_hbm, wq),
        local(4, go_hbm, go),
        local(5, wo_hbm, wo),
    ]
    for copy in loads:
        copy.start()

    barrier = pltpu.get_barrier_semaphore()
    for to in (peer, sib, near, far):
        pl.semaphore_signal(barrier, inc=1, device_id=to, device_id_type=MESH)
    pl.semaphore_wait(barrier, 4)

    def tp_copy(i, src, dst):
        return remote(src, dst, tp_ssem.at[i], tp_rsem.at[i], peer)

    tok_copy = tp_copy(0, tok_hbm, tokp)
    go_copy = tp_copy(1, go_hbm, gop)
    out_copy = tp_copy(2, osend, orecv)
    parts_of = [slice(0, BLK // 2), slice(BLK // 2, BLK)]
    in_copies = [tp_copy(3 + i, isend.at[part], irecv.at[part]) for i, part in enumerate(parts_of)]
    tok_copy.start()
    go_copy.start()

    def kv_copy(o, p):
        src = win.at[NEAR, p] if o == CROSS else kv_own.at[p]
        to = {SIB: sib, NEAR: far, FAR: near, CROSS: sib}[o]
        return remote(src, win.at[o, p], kv_ssem.at[o, p], kv_rsem.at[o, p], to)

    def sib_copy(p):
        return remote(gsib.at[p], rsib.at[p], g_ssem.at[0, p], g_rsem.at[0, p], sib)

    def far_copy(p):
        return remote(gfar.at[p], rnear.at[p], g_ssem.at[1, p], g_rsem.at[1, p], far)

    def near_copy(p):
        return remote(gnear.at[p], rfar.at[p], g_ssem.at[2, p], g_rsem.at[2, p], near)

    own_sky = sky_ref[s]
    near_sky = [nb_ref[j, own_sky] for j in range(3)]

    def around(offset):
        sky = sky_ref[(s + sgn * offset + n) % n]
        here = (sky == near_sky[0]) | (sky == near_sky[1]) | (sky == near_sky[2])
        return here, vc_ref[sky]

    own_count = vc_ref[own_sky]
    has_far, far_count = around(-2)
    has_cross, cross_count = around(-1)
    _, sib_count = around(1)
    has_near, near_count = around(2)
    c0 = has_far
    c1 = has_far & has_cross
    c2 = jnp.logical_not(has_near)
    counts = (
        own_count,
        jnp.where(c0, far_count, cross_count),
        jnp.where(c1, cross_count, sib_count),
        jnp.where(c2, sib_count, near_count),
    )
    rows = lax.broadcasted_iota(jnp.int32, (BLK, PAIR), 0)
    for j in range(4):
        bias[j * BLK : (j + 1) * BLK, :] = jnp.where(rows < counts[j], 0.0, -jnp.inf).astype(F32)

    own_rows = pl.ds(pl.multiple_of(t * HALF, HALF), HALF)
    peer_rows = pl.ds(pl.multiple_of((1 - t) * HALF, HALF), HALF)

    loads[0].wait()
    loads[1].wait()
    acc[0] = dot(tok[...], wk[own_rows, :])
    loads[2].wait()
    acc[1] = dot(tok[...], wv[own_rows, :])
    loads[3].wait()
    acc[2] = dot(tok[...], wq[own_rows, :])
    tok_copy.wait_recv()
    for half in range(2):
        cols = slice(half * 256, half * 256 + 256)
        for j, w in ((0, wk), (1, wv)):
            value = (acc[j, :, cols] + dot(tokp[...], w[peer_rows, cols])).astype(BF16)
            kv_own[2 * half, j] = value[:, :PAIR]
            kv_own[2 * half + 1, j] = value[:, PAIR:]
        for p in (2 * half, 2 * half + 1):
            for o, crosses in ((NEAR, far_crosses), (FAR, near_crosses)):
                pl.when(jnp.logical_not(crosses))(lambda o=o, p=p: kv_copy(o, p).start())
            kv_copy(SIB, p).start()

    first = lax.broadcasted_iota(jnp.int32, (BLK, PAIR), 1) < 64

    def split(ref, value):
        for p in range(NP):
            part = value[:, p * PAIR : (p + 1) * PAIR]
            ref[p, :BLK, :] = jnp.where(first, part, 0.0).astype(BF16)
            ref[p, BLK:, :] = jnp.where(first, 0.0, part).astype(BF16)

    split(q2, (acc[2] + dot(tokp[...], wq[peer_rows, :])) * 0.125)
    loads[4].wait()
    loads[5].wait()
    acc[0] = dot_nt(go[...], wo[:, own_rows])
    go_copy.wait_recv()

    for o, crosses in ((NEAR, far_crosses), (FAR, near_crosses)):

        @pl.when(crosses)
        def _():
            for p in range(NP):
                kv_copy(o, p).start()

    split(g2, acc[0] + dot_nt(gop[...], wo[:, peer_rows]))

    def forward_near(p):
        kv_copy(NEAR, p).wait_recv()
        kv_copy(CROSS, p).start()

    def combine_near(p):
        sib_copy(p).wait_recv()
        for j in range(2):
            gnear[p, j] = (near_g[p, j] + rsib[p, 1, j].astype(F32)).astype(BF16)

    def pair_step(p):
        kv_copy(SIB, p).wait_recv()
        kv_copy(FAR, p).wait_recv()
        kv_copy(CROSS, p).wait_recv()
        for j, ref in ((0, kc), (1, vc)):
            ref[0:256, :] = kv_own[p, j]
            ref[256:512, :] = pick(c0, win[FAR, p, j], win[CROSS, p, j])
            ref[512:768, :] = pick(c1, win[CROSS, p, j], win[SIB, p, j])
            ref[768:1024, :] = pick(c2, win[SIB, p, j], win[NEAR, p, j])
        q = q2[p]
        g = g2[p]
        for k in range(4):
            ks = slice(k * BLK, (k + 1) * BLK)
            b = bias[ks, :]
            s_ref[ks, :] = dot_nt(kc[ks, :], q) + jnp.concatenate([b, b, b, b], axis=1)
            d_ref[ks, :] = dot_nt(vc[ks, :], g)
        for c in range(4):
            cols = slice(c * 128, (c + 1) * 128)
            top = jnp.max(s_ref[:, cols], axis=0, keepdims=True)
            total = jnp.zeros((8, 128), F32)
            mixed = jnp.zeros((8, 128), F32)
            for k in range(8):
                ks = slice(k * 128, (k + 1) * 128)
                e = jnp.exp(s_ref[ks, cols] - top)
                s_ref[ks, cols] = e
                total = total + jnp.sum(e.reshape(16, 8, 128), axis=0)
                mixed = mixed + jnp.sum((e * d_ref[ks, cols]).reshape(16, 8, 128), axis=0)
            inverse = 1.0 / jnp.sum(total, axis=0, keepdims=True)
            delta = jnp.sum(mixed, axis=0, keepdims=True) * inverse
            for k in range(8):
                ks = slice(k * 128, (k + 1) * 128)
                prob = s_ref[ks, cols] * inverse
                p_ref[ks, cols] = prob.astype(BF16)
                ds_ref[ks, cols] = (prob * (d_ref[ks, cols] - delta)).astype(BF16)

        def parts(j, left, right):
            def block(b):
                return dot(left[b * BLK : (b + 1) * BLK, :], right)

            own_g[p, j] = block(0)
            a, b, c = block(1), block(2), block(3)
            zero = jnp.zeros_like(a)
            gfar[p, j] = pick(c0, a, zero).astype(BF16)
            gsib[p, 1, j] = pick(c0, pick(c1, b, zero), a).astype(BF16)
            gsib[p, 0, j] = pick(c1, pick(c2, c, zero), b).astype(BF16)
            near_g[p, j] = pick(c2, zero, c)

        between(p)
        parts(0, ds_ref, q)
        parts(1, p_ref, g)
        sib_copy(p).start()
        far_copy(p).start()
        lanes = pl.ds(pl.multiple_of(p * PAIR, PAIR), PAIR)
        for source, left, ref, scale in ((p_ref, vc, att, 1.0), (ds_ref, kc, dq, 0.125)):
            both = dot_tn(left[...], source[...])
            joined = jnp.concatenate([both[:64, :BLK], both[64:, BLK:]], axis=0) * scale
            ref[:, lanes] = joined.T.astype(BF16)

    forward_near(0)

    def finish(p):
        combine_near(p)
        near_copy(p).start()

    def between(p):
        @pl.when(p + 1 < NP)
        def _():
            forward_near(p + 1)

        @pl.when(p > 0)
        def _():
            finish(p - 1)

    @pl.loop(0, NP)
    def _(p):
        pair_step(p)

    finish(NP - 1)

    osend[...] = dot(att[...], wo[:, peer_rows]).astype(BF16)
    out_copy.start()
    acc[0] = dot(att[...], wo[:, own_rows])
    acc[1] = dot_nt(dq[...], wq[peer_rows, :])
    acc[2] = dot_nt(dq[...], wq[own_rows, :])

    for p in range(NP):
        far_copy(p).wait_recv()
        near_copy(p).wait_recv()
        lanes = slice(p * PAIR, (p + 1) * PAIR)
        for j, ref in ((0, dk), (1, dv)):
            summed = own_g[p, j] + rsib[p, 0, j].astype(F32)
            summed = summed + rnear[p, j].astype(F32) + rfar[p, j].astype(F32)
            ref[:, lanes] = summed.astype(BF16)
    for part, copy in zip(parts_of, in_copies):
        isend[part, :] = (
            acc[1, part, :] + dot_nt(dk[part, :], wk[peer_rows, :]) + dot_nt(dv[part, :], wv[peer_rows, :])
        ).astype(BF16)
        copy.start()
    out_copy.wait_recv()
    out_ref[...] = (acc[0] + orecv[...].astype(F32)).astype(BF16)
    acc[1] = acc[2] + dot_nt(dk[...], wk[own_rows, :]) + dot_nt(dv[...], wv[own_rows, :])
    for part, copy in zip(parts_of, in_copies):
        copy.wait_recv()
        ig_ref[part, :] = (acc[1, part, :] + irecv[part, :].astype(F32)).astype(BF16)

    for copy in (tok_copy, go_copy, out_copy, *in_copies):
        copy.wait_send()
    for p in range(NP):
        for o in range(4):
            kv_copy(o, p).wait_send()
        for copy in (sib_copy(p), far_copy(p), near_copy(p)):
            copy.wait_send()


def body(n, *args):
    args = args[:7] + (args[7].T,) + args[8:]
    args = args[:6] + tuple(pltpu.with_memory_space_constraint(x, pltpu.HBM) for x in args[6:])
    wide = (BLK, HALF)
    half = pltpu.VMEM(wide, BF16)
    weight = pltpu.VMEM((2 * HALF, HALF), BF16)
    pair_kv = pltpu.VMEM((NP, 2, BLK, PAIR), BF16)
    pair_f32 = pltpu.VMEM((NP, 2, BLK, PAIR), F32)
    sib_kv = pltpu.VMEM((NP, 2, 2, BLK, PAIR), BF16)
    scratch = [
        half, half, half, half, weight, weight, weight, pltpu.VMEM((HALF, 2 * HALF), BF16),
        pltpu.VMEM((3,) + wide, F32),
        pair_kv, pltpu.VMEM((4, NP, 2, BLK, PAIR), BF16),
        pltpu.VMEM((NP, 2 * BLK, PAIR), BF16), pltpu.VMEM((NP, 2 * BLK, PAIR), BF16),
        pltpu.VMEM((4 * BLK, PAIR), F32),
        pltpu.VMEM((4 * BLK, PAIR), BF16), pltpu.VMEM((4 * BLK, PAIR), BF16),
        pltpu.VMEM((4 * BLK, 2 * BLK), F32), pltpu.VMEM((4 * BLK, 2 * BLK), F32),
        pltpu.VMEM((4 * BLK, 2 * BLK), BF16), pltpu.VMEM((4 * BLK, 2 * BLK), BF16),
        half, half, pair_f32, pair_f32, sib_kv, pair_kv, pair_kv, sib_kv, pair_kv, pair_kv, half, half,
        half, half, half, half,
        pltpu.SemaphoreType.DMA((6,)),
        pltpu.SemaphoreType.DMA((5,)), pltpu.SemaphoreType.DMA((5,)),
        pltpu.SemaphoreType.DMA((4, NP)), pltpu.SemaphoreType.DMA((4, NP)),
        pltpu.SemaphoreType.DMA((3, NP)), pltpu.SemaphoreType.DMA((3, NP)),
    ]
    shape = jax.ShapeDtypeStruct(wide, BF16)
    return pl.pallas_call(
        functools.partial(kernel, n),
        name="sky_attention",
        out_shape=(shape, shape),
        in_specs=[pl.BlockSpec(memory_space=pltpu.HBM)] * 6 + [pl.BlockSpec(memory_space=pltpu.SMEM)] * 3,
        out_specs=[pl.BlockSpec(memory_space=pltpu.VMEM)] * 2,
        scratch_shapes=scratch,
        compiler_params=pltpu.CompilerParams(
            collective_id=0, has_side_effects=True, vmem_limit_bytes=213 << 18
        ),
    )(*args)


def solution(mesh):
    placed = (
        P("seq", "tp"),
        P(None, "tp"),
        P(None, "tp"),
        P(None, "tp"),
        P("tp", None),
        P("seq", "tp"),
        P(),
        P(),
        P(),
    )
    return jax.shard_map(
        functools.partial(body, mesh.shape["seq"]),
        mesh=mesh,
        in_specs=placed,
        out_specs=(P("seq", "tp"), P("seq", "tp")),
        check_vma=False,
    )
```
